128 devices in a mesh: plane: 8 (over y_hi, z), slab: 16 (over x, y_lo, core).
Axes of the slice: x: 4, y: 4 (y_hi: 2, y_lo: 2; y = y_hi * 2 + y_lo), z: 4, core: 2. Of those that a mesh axis runs over, the one named last changes fastest.
Arguments:
- potential: float32 [40, 96, 4096], P('plane', None, 'slab'), may hold values from -1.5 to 1.5
- mixing: float32 [40], P('plane'), may hold values from 1.05 to 1.6
- lens_weight: float32 [40], P('plane'), may hold values from 0.02 to 0.08
- observed: float32 [40, 3, 96, 4096], P('plane', None, 'slab'), may hold values from -6 to 6
- noise_weight: float32 [40, 96, 4096], P('plane', 'slab'), may hold values from 0.3 to 3
Outputs:
- deflection: float32 [40, 2, 96, 4096], P('plane', None, 'slab')
- shear: float32 [40, 3, 96, 4096], P('plane', None, 'slab')
- potential_grad: float32 [40, 96, 4096], P('plane', None, 'slab')
The draws below stay inside these ranges and needn't reach their ends.
All inputs are finite; a program needn't handle non-finite values.
Results may differ from the reference program's by a relative error of at most 0.00013.
Values sent between devices are 32-bit elements; how exact they have to be, the bound alone decides.
A program may use at most 256 MiB of HBM per device.

```python
import math
import jax
import jax.numpy as jnp
from jax import lax

W = 4096
PLANES = 40
NR = 96


def level_of(own_key, shape, cuts, smallest, high):
    def one(dim, shards_of):
        steps = jax.random.uniform(jax.random.fold_in(jax.random.fold_in(own_key, 6), dim), (shards_of,), jnp.float32, smallest / len(cuts), high / len(cuts))
        return jnp.repeat(jnp.exp(steps), shape[dim] // shards_of).reshape((-1,) + (1,) * (len(shape) - dim - 1))

    loudness = one(*cuts[0])
    for cut in cuts[1:]:
        loudness = loudness * one(*cut)
    return loudness


def noise(stream_key, dims, spread, limit, shards=(), dtype=jnp.bfloat16):
    entries = jax.random.normal(stream_key, dims, jnp.float32) * spread
    if len(shards) > 0:
        entries = level_of(stream_key, dims, shards, -0.22, 0.18) * entries
    return jnp.clip(entries, min=-limit, max=limit).astype(dtype)


def setup_inputs(seed: int = 0) -> dict:
    streams_of = jax.random.split(jax.random.key(seed), 6)
    return {
        "potential": noise(streams_of[0], (PLANES, NR, W), 0.25, 1.5, ((0, 8), (2, 16)), jnp.float32),
        "mixing": jnp.clip(jnp.exp(math.log(1.6) - 0.42121353 * jax.random.uniform(streams_of[1], (PLANES,), jnp.float32) ** level_of(streams_of[1], (PLANES,), ((0, 8),), -0.2, 0.2)), 1.05, 1.6),
        "lens_weight": jnp.clip(jnp.exp(math.log(0.08) - 1.3862944 * jax.random.uniform(streams_of[2], (PLANES,), jnp.float32) ** level_of(streams_of[2], (PLANES,), ((0, 8),), -0.2, 0.2)), 0.02, 0.08),
        "observed": noise(streams_of[3], (PLANES, 3, NR, W), 1.0, 6.0, ((0, 8), (2, 16)), jnp.float32),
        "noise_weight": jnp.clip(jnp.exp(math.log(3.0) - 2.3025851 * jax.random.uniform(streams_of[4], (PLANES, NR, W), jnp.float32) ** level_of(streams_of[4], (PLANES, NR, W), ((0, 8), (1, 16)), -0.2, 0.2)), 0.3, 3.0),
    }


def wrap_pad(array, dim):
    extent = array.shape[dim]
    leading = lax.slice_in_dim(array, 0, 1, axis=dim)
    trailing = lax.slice_in_dim(array, extent - 1, extent, axis=dim)
    return jnp.concatenate([trailing, array, leading], axis=dim)


def five_fields(padded):
    center = padded[..., 1:-1, 1:-1]
    row_next = padded[..., 2:, 1:-1]
    row_prev = padded[..., :-2, 1:-1]
    col_next = padded[..., 1:-1, 2:]
    col_prev = padded[..., 1:-1, :-2]
    mixed = 0.25 * (padded[..., 2:, 2:] - padded[..., 2:, :-2] - padded[..., :-2, 2:] + padded[..., :-2, :-2])
    return jnp.stack([0.5 * (row_next - row_prev), 0.5 * (col_next - col_prev),
                      row_next - 2.0 * center + row_prev, col_next - 2.0 * center + col_prev, mixed], axis=-3)


def adjoint_fields(padded):
    rows_part = padded[..., 0, 2:, 1:-1] - 2.0 * padded[..., 0, 1:-1, 1:-1] + padded[..., 0, :-2, 1:-1]
    cols_part = padded[..., 1, 1:-1, 2:] - 2.0 * padded[..., 1, 1:-1, 1:-1] + padded[..., 1, 1:-1, :-2]
    mixed_part = 0.25 * (padded[..., 2, 2:, 2:] - padded[..., 2, 2:, :-2] - padded[..., 2, :-2, 2:] + padded[..., 2, :-2, :-2])
    return rows_part + cols_part + mixed_part


def plane_forward(a_now, a_before, defl_now, defl_before, fields, mix, weight):
    diag_first = mix - weight * fields[2]
    diag_second = mix - weight * fields[3]
    off_diag = -weight * fields[4]
    keep = 1.0 - mix
    new_a = jnp.stack([diag_first * a_now[0] + off_diag * a_now[2] + keep * a_before[0],
                       diag_first * a_now[1] + off_diag * a_now[3] + keep * a_before[1],
                       off_diag * a_now[0] + diag_second * a_now[2] + keep * a_before[2],
                       off_diag * a_now[1] + diag_second * a_now[3] + keep * a_before[3]])
    new_defl = mix * defl_now + keep * defl_before - weight * fields[0:2]
    return new_a, new_defl


def shear_of(distort):
    return jnp.stack([1.0 - 0.5 * (distort[0] + distort[3]), 0.5 * (distort[3] - distort[0]), -0.5 * (distort[1] + distort[2])])


def source_adjoint(residual):
    return jnp.stack([-0.5 * (residual[..., 0, :, :] + residual[..., 1, :, :]), -0.5 * residual[..., 2, :, :],
                      -0.5 * residual[..., 2, :, :], -0.5 * (residual[..., 0, :, :] - residual[..., 1, :, :])], axis=-3)


def plane_adjoint(p_full, q_state, a_now, fields, mix, weight):
    diag_first = mix - weight * fields[2]
    diag_second = mix - weight * fields[3]
    off_diag = -weight * fields[4]
    keep = 1.0 - mix
    new_p = jnp.stack([diag_first * p_full[0] + off_diag * p_full[2],
                       diag_first * p_full[1] + off_diag * p_full[3],
                       off_diag * p_full[0] + diag_second * p_full[2],
                       off_diag * p_full[1] + diag_second * p_full[3]]) + q_state
    new_q = keep * p_full
    cot = jnp.stack([-weight * (p_full[0] * a_now[0] + p_full[1] * a_now[1]),
                     -weight * (p_full[2] * a_now[2] + p_full[3] * a_now[3]),
                     -weight * (p_full[0] * a_now[2] + p_full[1] * a_now[3] + p_full[2] * a_now[0] + p_full[3] * a_now[1])])
    return new_p, new_q, cot


def reference(potential, mixing, lens_weight, observed, noise_weight):
    fields = five_fields(wrap_pad(wrap_pad(potential, 1), 2))
    map_shape = potential.shape[1:]
    ones_map = jnp.ones(map_shape, jnp.float32)
    zeros_map = jnp.zeros(map_shape, jnp.float32)
    a_now = jnp.stack([ones_map, zeros_map, zeros_map, ones_map])
    a_before = a_now
    defl_now = jnp.zeros((2,) + map_shape, jnp.float32)
    defl_before = defl_now
    stored = []
    deflections = []
    shears = []
    for plane_index in range(PLANES):
        stored.append(a_now)
        new_a, new_defl = plane_forward(a_now, a_before, defl_now, defl_before, fields[plane_index],
                                        mixing[plane_index], lens_weight[plane_index])
        a_before, a_now = a_now, new_a
        defl_before, defl_now = defl_now, new_defl
        deflections.append(new_defl)
        shears.append(shear_of(new_a))
    deflection = jnp.stack(deflections)
    shear = jnp.stack(shears)
    residual = noise_weight[:, None] * (shear - observed)
    sources = source_adjoint(residual)
    p_state = jnp.zeros((4,) + map_shape, jnp.float32)
    q_state = jnp.zeros((4,) + map_shape, jnp.float32)
    cotangents = [None] * PLANES
    for plane_index in reversed(range(PLANES)):
        p_full = p_state + sources[plane_index]
        p_state, q_state, cotangents[plane_index] = plane_adjoint(p_full, q_state, stored[plane_index], fields[plane_index],
                                                                  mixing[plane_index], lens_weight[plane_index])
    cot = jnp.stack(cotangents)
    potential_grad = adjoint_fields(wrap_pad(wrap_pad(cot, 2), 3))
    return deflection, shear, potential_grad
```

```python
import functools

import jax
import jax.numpy as jnp
from jax import lax
from jax.experimental import pallas as pl
from jax.experimental.pallas import tpu as pltpu
from jax.sharding import PartitionSpec as P

F32 = jnp.float32
MESH = pl.DeviceIdType.MESH
NH = 2


def rows_of(x, shift):
    return pltpu.roll(x, (-shift) % 8, axis=0)


def cols_of(x, shift):
    return pltpu.roll(x, (-shift) % 128, axis=1)


def iotas():
    return (
        lax.broadcasted_iota(jnp.int32, (8, 128), 0),
        lax.broadcasted_iota(jnp.int32, (8, 128), 1),
    )


def pack4(tiles, sub):
    a, b, c, d = tiles
    return jnp.concatenate(
        [
            jnp.where(sub < 6, a, rows_of(d, -6)),
            jnp.where(sub < 6, b, rows_of(d, -4)),
            jnp.where(sub < 6, c, rows_of(d, -2)),
        ],
        axis=0,
    )


def unpack4(x, sub):
    a, b, c = x[0:8], x[8:16], x[16:24]
    d = jnp.where(
        sub < 2, rows_of(a, -2), jnp.where(sub < 4, rows_of(b, -4), rows_of(c, -6))
    )
    return [a, b, c, d]


def neighbours(tiles, left, right, lane):
    ahead = [cols_of(t, -1) for t in tiles]
    behind = [cols_of(t, 1) for t in tiles]
    n = len(tiles)
    lefts = [jnp.where(lane == 0, left if i == 0 else ahead[i - 1], ahead[i]) for i in range(n)]
    rights = [
        jnp.where(lane == 127, right if i == n - 1 else behind[i + 1], behind[i]) for i in range(n)
    ]
    return lefts, rights


def bends(t, lf, rt):
    mid = rows_of(t, 1)
    down = rows_of(t, 2)
    rr = down - 2.0 * mid + t
    cc = rows_of(rt - 2.0 * t + lf, 1)
    q = 0.25 * (rt - lf)
    return rr, cc, rows_of(q, 2) - q


def slopes(t, lf, rt):
    return 0.5 * (rows_of(t, 2) - t), rows_of(0.5 * (rt - lf), 1)


def step_forward(now, before, d1, d2, off, keep):
    return [
        d1 * now[0] + off * now[2] + keep * before[0],
        d1 * now[1] + off * now[3] + keep * before[1],
        off * now[0] + d2 * now[2] + keep * before[2],
        off * now[1] + d2 * now[3] + keep * before[3],
    ]


def shear_of(a):
    return [1.0 - 0.5 * (a[0] + a[3]), 0.5 * (a[3] - a[0]), -0.5 * (a[1] + a[2])]


def kernel(
    nz, ns, nk,
    pot, mix_in, wgt_in, obs, noi,
    defl, shear, grad,
    pv, ov, nv, psend, esend, msend, osend,
    prx, erx, mrx, prow, orx,
    ast, mst, phi, sta, stp, pq,
    gsend, gesend, grx, gerx, dv, sv, gv,
    lsem, ps, es, ms, os_, rs, sas, sps, cs, gs, ges, rsem, osem,
):
    h = lax.axis_index("plane") // nz
    z = lax.axis_index("plane") % nz
    s = lax.axis_index("slab")
    per = ns // nz
    blk = s // per
    pos = s % per
    sub, lane = iotas()

    load_p = pltpu.make_async_copy(pot, pv, lsem.at[0])
    load_o = pltpu.make_async_copy(obs, ov, lsem.at[1])
    load_n = pltpu.make_async_copy(noi, nv, lsem.at[2])
    load_p.start()
    load_o.start()
    load_n.start()

    barrier = pltpu.get_barrier_semaphore()

    @pl.loop(0, nz * ns)
    def _(i):
        zz = i // ns
        ss = i % ns

        @pl.when((zz != z) | (ss != s))
        def _():
            pl.semaphore_signal(
                barrier, inc=1, device_id={"plane": h * nz + zz, "slab": ss}, device_id_type=MESH
            )

    pl.semaphore_signal(
        barrier, inc=1, device_id={"plane": (1 - h) * nz + z, "slab": s}, device_id_type=MESH
    )

    def remote(src, dst, ssem, r, zz, ss):
        return pltpu.make_async_remote_copy(
            src_ref=src, dst_ref=dst, send_sem=ssem, recv_sem=r,
            device_id={"plane": h * nz + zz, "slab": ss}, device_id_type=MESH,
        )

    def send(src, dst, ssem, r, zz, ss):
        own = (zz == z) & (ss == s)

        @pl.when(jnp.logical_not(own))
        def _():
            remote(src, dst, ssem, r, zz, ss).start()

        @pl.when(own)
        def _():
            pltpu.make_async_copy(src, dst, r).start()

    def sent(src, dst, ssem, r, zz, ss):
        @pl.when((zz != z) | (ss != s))
        def _():
            remote(src, dst, ssem, r, zz, ss).wait_send()

    def arrived(buf, r):
        pltpu.make_async_copy(buf, buf, r).wait()

    load_p.wait()
    total = 6 * ns
    for d in range(ns):
        edge = jnp.zeros((8, 128), F32)
        for k in range(nk):
            for t in range(2):
                cols = pl.ds(128 * t, 128)
                if d == 0:
                    v = jnp.where(
                        sub == 0, pv[k, total - 8:total, cols][7:8], rows_of(pv[k, 0:8, cols], -1)
                    )
                elif d == ns - 1:
                    v = jnp.where(
                        sub == 7, pv[k, 0:8, cols][0:1], rows_of(pv[k, total - 8:total, cols], 1)
                    )
                else:
                    v = pv[k, 6 * d - 1:6 * d + 7, cols]
                psend[d, k, :, cols] = v
                if t == 0:
                    first = jnp.broadcast_to(v[:, 0:1], (8, 128))
                else:
                    last = jnp.broadcast_to(v[:, 127:128], (8, 128))
            edge = jnp.where(lane == k, jnp.where(pos == 0, first, last), edge)
        esend[d] = edge
    for k in range(nk):
        msend[k:k + 1, :] = jnp.full((1, 128), mix_in[k], F32)
        msend[8 + k:9 + k, :] = jnp.full((1, 128), wgt_in[k], F32)

    pl.semaphore_wait(barrier, nz * ns)

    eblk = jnp.where(pos == 0, (blk + nz - 1) % nz, (blk + 1) % nz)
    eside = jnp.where(pos == 0, 1, 0)
    on_edge = (pos == 0) | (pos == per - 1)

    def each(n, fn, args):
        @pl.loop(0, n)
        def _(i):
            fn(*args(i))

    pix_args = lambda d: (psend.at[d], prx.at[z, pos], ps.at[0, d], rsem.at[0], blk, d)
    row_args = lambda d: (psend.at[d], prow.at[s], ps.at[1, d], rsem.at[1], z, d)
    edge_args = lambda d: (esend.at[d], erx.at[z, eside], es.at[d], rsem.at[2], eblk, d)
    meta_args = lambda d: (msend, mrx.at[z], ms.at[d], rsem.at[3], d, s)
    obs_args = lambda d: (osend.at[d], orx.at[z], os_.at[d], osem.at[z], d, s)

    each(ns, send, pix_args)

    @pl.when(on_edge)
    def _():
        each(ns, send, edge_args)

    each(nz, send, meta_args)

    load_o.wait()
    load_n.wait()

    @pl.loop(0, nz)
    def _(d):
        for k in range(nk):
            for a in range(4):
                for hb in range(2):
                    t = []
                    for i in range(4):
                        c = pl.ds(pl.multiple_of(d * 1024 + (hb * 4 + i) * 128, 128), 128)
                        t.append(ov[k, a, :, c] if a < 3 else nv[k, :, c])
                    for i in range(3):
                        osend[d, k, a, hb, pl.ds(8 * i, 8), :] = jnp.concatenate(
                            [t[i], t[3][2 * i:2 * i + 2]], axis=0
                        )

    each(nz, send, obs_args)
    each(ns, send, row_args)

    @pl.when(h == 0)
    def _():
        one = jnp.ones((2, 24, 128), F32)
        zero = jnp.zeros((2, 24, 128), F32)
        for i in range(2):
            ast[i, 0] = one
            ast[i, 1] = zero
            ast[i, 2] = zero
            ast[i, 3] = one
            phi[i] = jnp.zeros((8, 8, 128), F32)

    arrived(prx, rsem.at[0])
    arrived(erx, rsem.at[2])
    arrived(mrx, rsem.at[3])

    last = nz * nk

    def chain_copy(buf, i, r):
        return pltpu.make_async_remote_copy(
            src_ref=buf.at[pl.ds(last, 2)], dst_ref=buf.at[pl.ds(0, 2)],
            send_sem=cs.at[i], recv_sem=r,
            device_id={"plane": nz + z, "slab": s}, device_id_type=MESH,
        )

    @pl.when(h == 1)
    def _():
        arrived(ast.at[pl.ds(0, 2)], rsem.at[4])
        arrived(phi.at[pl.ds(0, 2)], rsem.at[5])

    sta_args = lambda q: (ast.at[pl.ds(nk * q, 2)], sta.at[z], sas.at[q], rsem.at[6], q, s)
    stp_args = lambda q: (phi.at[pl.ds(nk * q, 2)], stp.at[z], sps.at[q], rsem.at[7], q, s)

    @pl.loop(0, nz)
    def _(zz):
        for k in range(nk):
            kk = zz * nk + k
            mix = jnp.broadcast_to(mrx[zz, k:k + 1, :], (8, 128))
            wgt = jnp.broadcast_to(mrx[zz, 8 + k:9 + k, :], (8, 128))
            keep = 1.0 - mix
            mix3 = jnp.concatenate([mix] * 3, axis=0)
            wgt3 = jnp.concatenate([wgt] * 3, axis=0)
            keep3 = 1.0 - mix3
            left = jnp.broadcast_to(erx[zz, 0][:, k:k + 1], (8, 128))
            right = jnp.broadcast_to(erx[zz, 1][:, k:k + 1], (8, 128))
            tiles = [prx[zz, i // 2, k, :, pl.ds(128 * (i % 2), 128)] for i in range(8)]
            lefts, rights = neighbours(tiles, left, right, lane)
            for i in range(8):
                phi[kk + 2, i] = mix * phi[kk + 1, i] + keep * phi[kk, i] - wgt * tiles[i]
            for hb in range(2):
                b = [bends(tiles[i], lefts[i], rights[i]) for i in range(4 * hb, 4 * hb + 4)]
                d1 = mix3 - wgt3 * pack4([x[0] for x in b], sub)
                d2 = mix3 - wgt3 * pack4([x[1] for x in b], sub)
                off = -wgt3 * pack4([x[2] for x in b], sub)
                mst[kk, 0, hb] = d1
                mst[kk, 1, hb] = d2
                mst[kk, 2, hb] = off
                now = [ast[kk + 1, c, hb] for c in range(4)]
                before = [ast[kk, c, hb] for c in range(4)]
                new = step_forward(now, before, d1, d2, off, keep3)
                for c in range(4):
                    ast[kk + 2, c, hb] = new[c]
        send(*sta_args(zz))
        send(*stp_args(zz))

    @pl.when(h == 0)
    def _():
        chain_copy(ast, 0, rsem.at[4]).start()
        chain_copy(phi, 1, rsem.at[5]).start()

    def back_copy():
        return pltpu.make_async_remote_copy(
            src_ref=pq.at[0], dst_ref=pq.at[1], send_sem=cs.at[2], recv_sem=rsem.at[8],
            device_id={"plane": z, "slab": s}, device_id_type=MESH,
        )

    @pl.when(h == 1)
    def _():
        pq[0] = jnp.zeros(pq.shape[1:], F32)

    for d in range(nz):
        arrived(orx.at[d], osem.at[d])

    @pl.when(h == 0)
    def _():
        arrived(pq.at[1], rsem.at[8])
        pq[0] = pq[1]

    g_args = lambda zz, j: (
        gsend.at[zz, j], grx.at[s], gs.at[zz, j], rsem.at[9], zz, z * per + j
    )
    gl_args = lambda zz: (
        gesend.at[zz, 0], gerx.at[s], ges.at[zz, 0], rsem.at[10], zz, (z * per + ns - 1) % ns
    )
    gr_args = lambda zz: (
        gesend.at[zz, 1], gerx.at[s], ges.at[zz, 1], rsem.at[10], zz, (z * per + per) % ns
    )

    zero8 = jnp.zeros((8, 128), F32)
    inner = (sub >= 1) & (sub <= 6)

    @pl.loop(0, nz)
    def _(back):
        zz = nz - 1 - back
        el = zero8
        er = zero8
        for k in reversed(range(nk)):
            kk = zz * nk + k
            mix = jnp.broadcast_to(mrx[zz, k:k + 1, :], (24, 128))
            wgt = jnp.broadcast_to(mrx[zz, 8 + k:9 + k, :], (24, 128))
            keep = 1.0 - mix
            c0, c1, c2 = [], [], []
            for hb in range(2):
                nxt = [ast[kk + 2, c, hb] for c in range(4)]
                a = [ast[kk + 1, c, hb] for c in range(4)]
                nw = orx[zz, k, 3, hb]
                r = [nw * (m - orx[zz, k, c, hb]) for c, m in enumerate(shear_of(nxt))]
                tilt = -0.5 * r[2]
                f = [
                    pq[0, 0, hb] - 0.5 * (r[0] + r[1]),
                    pq[0, 1, hb] + tilt,
                    pq[0, 2, hb] + tilt,
                    pq[0, 3, hb] - 0.5 * (r[0] - r[1]),
                ]
                d1, d2, off = mst[kk, 0, hb], mst[kk, 1, hb], mst[kk, 2, hb]
                pq[0, 0, hb] = d1 * f[0] + off * f[2] + pq[0, 4, hb]
                pq[0, 1, hb] = d1 * f[1] + off * f[3] + pq[0, 5, hb]
                pq[0, 2, hb] = off * f[0] + d2 * f[2] + pq[0, 6, hb]
                pq[0, 3, hb] = off * f[1] + d2 * f[3] + pq[0, 7, hb]
                for c in range(4):
                    pq[0, 4 + c, hb] = keep * f[c]
                nwt = -wgt
                c0 += unpack4(nwt * (f[0] * a[0] + f[1] * a[1]), sub)
                c1 += unpack4(nwt * (f[2] * a[2] + f[3] * a[3]), sub)
                c2 += unpack4(nwt * (f[0] * a[2] + f[1] * a[3] + f[2] * a[0] + f[3] * a[1]), sub)
            c0 = [jnp.where(inner, rows_of(t, -1), 0.0) for t in c0]
            c1 = [jnp.where(inner, rows_of(t, -1), 0.0) for t in c1]
            c2 = [jnp.where(inner, rows_of(t, -1), 0.0) for t in c2]
            l1, r1 = neighbours(c1, zero8, zero8, lane)
            l2, r2 = neighbours(c2, zero8, zero8, lane)
            for i in range(8):
                q = 0.25 * (r2[i] - l2[i])
                g = (
                    rows_of(c0[i], 1) - 2.0 * c0[i] + rows_of(c0[i], -1)
                    + (r1[i] - 2.0 * c1[i] + l1[i])
                    + (rows_of(q, 1) - rows_of(q, -1))
                )
                gsend[zz, i // 2, k, :, pl.ds(128 * (i % 2), 128)] = g
            vl = c1[0] + 0.25 * (rows_of(c2[0], 1) - rows_of(c2[0], -1))
            vr = c1[7] - 0.25 * (rows_of(c2[7], 1) - rows_of(c2[7], -1))
            el = jnp.where(lane == k, jnp.broadcast_to(vl[:, 0:1], (8, 128)), el)
            er = jnp.where(lane == k, jnp.broadcast_to(vr[:, 127:128], (8, 128)), er)
        gesend[zz, 0] = el
        gesend[zz, 1] = er
        for j in range(per):
            send(*g_args(zz, j))
        send(*gl_args(zz))
        send(*gr_args(zz))

    @pl.when(h == 1)
    def _():
        back_copy().start()

    arrived(prow, rsem.at[1])
    arrived(sta, rsem.at[6])
    arrived(stp, rsem.at[7])
    nchunk = 2 * nz

    @pl.loop(0, nchunk)
    def _(m):
        c = m // 2
        hb = m % 2
        cp = ((m + nchunk - 1) % nchunk) // 2
        cn = ((m + 1) % nchunk) // 2
        tp = (4 * hb + 7) % 8
        tn = (4 * hb + 4) % 8
        y = []
        for b in range(2):
            t = [stp[c, b, 4 * hb + i] for i in range(4)]
            lf, rt = neighbours(
                t, cols_of(stp[cp, b, tp], -1), cols_of(stp[cn, b, tn], 1), lane
            )
            y.append([slopes(t[i], lf[i], rt[i]) for i in range(4)])
        ybefore, ynow = y
        before = [sta[c, 0, e, hb] for e in range(4)]
        now = [sta[c, 1, e, hb] for e in range(4)]
        for k in range(nk):
            mix = mix_in[k]
            wgt = wgt_in[k]
            keep = 1.0 - mix
            t = [
                prow[2 * m + i // 2, k, :, pl.ds(128 * (i % 2), 128)] for i in range(4)
            ]
            left = cols_of(prow[(2 * m + ns - 1) % ns, k, :, pl.ds(128, 128)], -1)
            right = cols_of(prow[(2 * m + 2) % ns, k, :, pl.ds(0, 128)], 1)
            lf, rt = neighbours(t, left, right, lane)
            b = [bends(t[i], lf[i], rt[i]) for i in range(4)]
            d1 = mix - wgt * pack4([x[0] for x in b], sub)
            d2 = mix - wgt * pack4([x[1] for x in b], sub)
            off = -wgt * pack4([x[2] for x in b], sub)
            new = step_forward(now, before, d1, d2, off, keep)
            before, now = now, new
            for e, x in enumerate(shear_of(new)):
                for i, part in enumerate(unpack4(x, sub)):
                    col = pl.ds(pl.multiple_of(m * 512 + i * 128, 128), 128)
                    sv[k, e, :, col] = part[0:6]
            ynew = []
            for i in range(4):
                sl = slopes(t[i], lf[i], rt[i])
                both = []
                for e in range(2):
                    v = mix * ynow[i][e] + keep * ybefore[i][e] - wgt * sl[e]
                    both.append(v)
                    col = pl.ds(pl.multiple_of(m * 512 + i * 128, 128), 128)
                    dv[k, e, :, col] = v[0:6]
                ynew.append(both)
            ybefore, ynow = ynow, ynew

    out_s = pltpu.make_async_copy(sv, shear, lsem.at[3])
    out_d = pltpu.make_async_copy(dv, defl, lsem.at[4])
    out_s.start()
    out_d.start()

    arrived(grx, rsem.at[9])

    @pl.when(on_edge)
    def _():
        arrived(gerx, rsem.at[10])

    @pl.when(pos == 0)
    def _():
        for d in range(ns):
            for k in range(nk):
                e = jnp.broadcast_to(gerx[d][:, k:k + 1], (8, 128))
                grx[d, k, :, 0:128] = grx[d, k, :, 0:128] + jnp.where(lane == 0, e, 0.0)

    @pl.when(pos == per - 1)
    def _():
        for d in range(ns):
            for k in range(nk):
                e = jnp.broadcast_to(gerx[d][:, k:k + 1], (8, 128))
                grx[d, k, :, 128:256] = grx[d, k, :, 128:256] + jnp.where(lane == 127, e, 0.0)

    for d in range(ns):
        for k in range(nk):
            for t in range(2):
                col = pl.ds(128 * t, 128)
                g = grx[d, k, :, col]
                g = g + jnp.where(sub == 1, rows_of(grx[(d + ns - 1) % ns, k, :, col], 6), 0.0)
                g = g + jnp.where(sub == 6, rows_of(grx[(d + 1) % ns, k, :, col], -6), 0.0)
                gv[k, 6 * d:6 * d + 6, col] = rows_of(g, 1)[0:6]
    out_g = pltpu.make_async_copy(gv, grad, lsem.at[5])
    out_g.start()

    each(ns, sent, pix_args)
    each(ns, sent, row_args)

    @pl.when(on_edge)
    def _():
        each(ns, sent, edge_args)

    each(nz, sent, meta_args)
    each(nz, sent, obs_args)
    each(nz, sent, sta_args)
    each(nz, sent, stp_args)

    @pl.when(h == 0)
    def _():
        chain_copy(ast, 0, rsem.at[4]).wait_send()
        chain_copy(phi, 1, rsem.at[5]).wait_send()

    @pl.when(h == 1)
    def _():
        back_copy().wait_send()

    @pl.loop(0, nz)
    def _(zz):
        for j in range(per):
            sent(*g_args(zz, j))
        sent(*gl_args(zz))
        sent(*gr_args(zz))

    out_s.wait()
    out_d.wait()
    out_g.wait()


def on_device(nz, ns, potential, mixing, lens_weight, observed, noise_weight):
    nk, total, width = potential.shape
    rows = total // ns
    wide = ns * width
    per = ns // nz
    last = nz * nk
    anyspec = pl.BlockSpec(memory_space=pl.ANY)
    smem = pl.BlockSpec(memory_space=pltpu.SMEM)
    v = lambda *shape: pltpu.VMEM(shape, F32)
    dma = lambda *shape: pltpu.SemaphoreType.DMA(shape)
    return pl.pallas_call(
        functools.partial(kernel, nz, ns, nk),
        out_shape=(
            jax.ShapeDtypeStruct((nk, 2, rows, wide), F32),
            jax.ShapeDtypeStruct((nk, 3, rows, wide), F32),
            jax.ShapeDtypeStruct((nk, total, width), F32),
        ),
        in_specs=[anyspec, smem, smem, anyspec, anyspec],
        out_specs=(anyspec, anyspec, anyspec),
        scratch_shapes=[
            v(nk, total, width), v(nk, 3, rows, wide), v(nk, rows, wide),
            v(ns, nk, 8, width), v(ns, 8, 128), v(16, 128), v(nz, nk, 4, 2, 24, 128),
            v(nz, per, nk, 8, width), v(nz, 2, 8, 128), v(nz, 16, 128),
            v(ns, nk, 8, width), v(nz, nk, 4, 2, 24, 128),
            v(last + 2, 4, 2, 24, 128), v(last, 3, 2, 24, 128), v(last + 2, 8, 8, 128),
            v(nz, 2, 4, 2, 24, 128), v(nz, 2, 8, 8, 128), v(2, 8, 2, 24, 128),
            v(nz, per, nk, 8, width), v(nz, 2, 8, 128), v(ns, nk, 8, width), v(ns, 8, 128),
            v(nk, 2, rows, wide), v(nk, 3, rows, wide), v(nk, total, width),
            dma(6), dma(2, ns), dma(ns), dma(nz), dma(nz), dma(1), dma(nz), dma(nz), dma(3),
            dma(nz, per), dma(nz, 2), dma(11), dma(nz),
        ],
        name="lens",
        compiler_params=pltpu.CompilerParams(
            collective_id=0, has_side_effects=True, vmem_limit_bytes=60 * 1024 * 1024
        ),
    )(potential, mixing, lens_weight, observed, noise_weight)


def solution(mesh):
    nz = mesh.shape["plane"] // NH
    ns = mesh.shape["slab"]
    placed = (
        P("plane", None, "slab"),
        P("plane"),
        P("plane"),
        P("plane", None, "slab", None),
        P("plane", "slab", None),
    )
    return jax.shard_map(
        functools.partial(on_device, nz, ns),
        mesh=mesh,
        in_specs=placed,
        out_specs=(
            P("plane", None, "slab", None),
            P("plane", None, "slab", None),
            P("plane", None, "slab"),
        ),
        check_vma=False,
    )
```

```python
import functools

import jax
import jax.numpy as jnp
from jax import lax
from jax.experimental import pallas as pl
from jax.experimental.pallas import tpu as pltpu
from jax.sharding import PartitionSpec as P

F32 = jnp.float32
MESH = pl.DeviceIdType.MESH
NH = 2


def rows_of(x, shift):
    return pltpu.roll(x, (-shift) % 8, axis=0)


def cols_of(x, shift):
    return pltpu.roll(x, (-shift) % 128, axis=1)


def iotas():
    return (
        lax.broadcasted_iota(jnp.int32, (8, 128), 0),
        lax.broadcasted_iota(jnp.int32, (8, 128), 1),
    )


def pack4(tiles, sub):
    a, b, c, d = tiles
    return jnp.concatenate(
        [
            jnp.where(sub < 6, a, rows_of(d, -6)),
            jnp.where(sub < 6, b, rows_of(d, -4)),
            jnp.where(sub < 6, c, rows_of(d, -2)),
        ],
        axis=0,
    )


def unpack4(x, sub):
    a, b, c = x[0:8], x[8:16], x[16:24]
    d = jnp.where(
        sub < 2, rows_of(a, -2), jnp.where(sub < 4, rows_of(b, -4), rows_of(c, -6))
    )
    return [a, b, c, d]


def neighbours(tiles, left, right, lane):
    ahead = [cols_of(t, -1) for t in tiles]
    behind = [cols_of(t, 1) for t in tiles]
    n = len(tiles)
    lefts = [jnp.where(lane == 0, left if i == 0 else ahead[i - 1], ahead[i]) for i in range(n)]
    rights = [
        jnp.where(lane == 127, right if i == n - 1 else behind[i + 1], behind[i]) for i in range(n)
    ]
    return lefts, rights


def bends(t, lf, rt):
    mid = rows_of(t, 1)
    down = rows_of(t, 2)
    rr = down - 2.0 * mid + t
    cc = rows_of(rt - 2.0 * t + lf, 1)
    q = 0.25 * (rt - lf)
    return rr, cc, rows_of(q, 2) - q


def slopes(t, lf, rt):
    return 0.5 * (rows_of(t, 2) - t), rows_of(0.5 * (rt - lf), 1)


def step_forward(now, before, d1, d2, off, keep):
    return [
        d1 * now[0] + off * now[2] + keep * before[0],
        d1 * now[1] + off * now[3] + keep * before[1],
        off * now[0] + d2 * now[2] + keep * before[2],
        off * now[1] + d2 * now[3] + keep * before[3],
    ]


def shear_of(a):
    return [1.0 - 0.5 * (a[0] + a[3]), 0.5 * (a[3] - a[0]), -0.5 * (a[1] + a[2])]


def kernel(
    nz, ns, nk,
    pot, mix_in, wgt_in, obs, noi,
    defl, shear, grad,
    pv, ov, nv, psend, esend, msend, osend,
    prx, erx, mrx, prow, orx,
    ast, mst, phi, sta, stp, pq,
    gsend, gesend, gmid, gemid, grx, gerx, dv, sv, gv,
    lsem, ps, es, ms, os_, rs, sas, sps, cs, gs, ges, fs, fes, rsem, osem, gsem, gesem,
):
    h = lax.axis_index("plane") // nz
    z = lax.axis_index("plane") % nz
    s = lax.axis_index("slab")
    per = ns // nz
    blk = s // per
    pos = s % per
    sub, lane = iotas()

    load_p = pltpu.make_async_copy(pot, pv, lsem.at[0])
    load_o = pltpu.make_async_copy(obs, ov, lsem.at[1])
    load_n = pltpu.make_async_copy(noi, nv, lsem.at[2])
    load_p.start()
    load_o.start()
    load_n.start()

    barrier = pltpu.get_barrier_semaphore()

    @pl.loop(0, nz * ns)
    def _(i):
        zz = i // ns
        ss = i % ns

        @pl.when((zz != z) | (ss != s))
        def _():
            pl.semaphore_signal(
                barrier, inc=1, device_id={"plane": h * nz + zz, "slab": ss}, device_id_type=MESH
            )

    pl.semaphore_signal(
        barrier, inc=1, device_id={"plane": (1 - h) * nz + z, "slab": s}, device_id_type=MESH
    )

    def remote(src, dst, ssem, r, zz, ss):
        return pltpu.make_async_remote_copy(
            src_ref=src, dst_ref=dst, send_sem=ssem, recv_sem=r,
            device_id={"plane": h * nz + zz, "slab": ss}, device_id_type=MESH,
        )

    def send(src, dst, ssem, r, zz, ss):
        own = (zz == z) & (ss == s)

        @pl.when(jnp.logical_not(own))
        def _():
            remote(src, dst, ssem, r, zz, ss).start()

        @pl.when(own)
        def _():
            pltpu.make_async_copy(src, dst, r).start()

    def sent(src, dst, ssem, r, zz, ss):
        @pl.when((zz != z) | (ss != s))
        def _():
            remote(src, dst, ssem, r, zz, ss).wait_send()

    def arrived(buf, r):
        pltpu.make_async_copy(buf, buf, r).wait()

    load_p.wait()
    total = 6 * ns
    for d in range(ns):
        edge = jnp.zeros((8, 128), F32)
        for k in range(nk):
            for t in range(2):
                cols = pl.ds(128 * t, 128)
                if d == 0:
                    v = jnp.where(
                        sub == 0, pv[k, total - 8:total, cols][7:8], rows_of(pv[k, 0:8, cols], -1)
                    )
                elif d == ns - 1:
                    v = jnp.where(
                        sub == 7, pv[k, 0:8, cols][0:1], rows_of(pv[k, total - 8:total, cols], 1)
                    )
                else:
                    v = pv[k, 6 * d - 1:6 * d + 7, cols]
                psend[d, k, :, cols] = v
                if t == 0:
                    first = jnp.broadcast_to(v[:, 0:1], (8, 128))
                else:
                    last = jnp.broadcast_to(v[:, 127:128], (8, 128))
            edge = jnp.where(lane == k, jnp.where(pos == 0, first, last), edge)
        esend[d] = edge
    for k in range(nk):
        msend[k:k + 1, :] = jnp.full((1, 128), mix_in[k], F32)
        msend[8 + k:9 + k, :] = jnp.full((1, 128), wgt_in[k], F32)

    pl.semaphore_wait(barrier, nz * ns)

    eblk = jnp.where(pos == 0, (blk + nz - 1) % nz, (blk + 1) % nz)
    eside = jnp.where(pos == 0, 1, 0)
    on_edge = (pos == 0) | (pos == per - 1)

    def each(n, fn, args):
        @pl.loop(0, n)
        def _(i):
            fn(*args(i))

    pix_args = lambda d: (psend.at[d], prx.at[z, pos], ps.at[0, d], rsem.at[0], blk, d)
    row_args = lambda d: (psend.at[d], prow.at[s], ps.at[1, d], rsem.at[1], z, d)
    edge_args = lambda d: (esend.at[d], erx.at[z, eside], es.at[d], rsem.at[2], eblk, d)
    meta_args = lambda d: (msend, mrx.at[z], ms.at[d], rsem.at[3], d, s)
    obs_args = lambda d: (osend.at[d], orx.at[z], os_.at[d], osem.at[z], d, s)

    each(ns, send, pix_args)

    @pl.when(on_edge)
    def _():
        each(ns, send, edge_args)

    each(nz, send, meta_args)

    load_o.wait()
    load_n.wait()

    @pl.loop(0, nz)
    def _(d):
        for k in range(nk):
            for a in range(4):
                for hb in range(2):
                    t = []
                    for i in range(4):
                        c = pl.ds(pl.multiple_of(d * 1024 + (hb * 4 + i) * 128, 128), 128)
                        t.append(ov[k, a, :, c] if a < 3 else nv[k, :, c])
                    for i in range(3):
                        osend[d, k, a, hb, pl.ds(8 * i, 8), :] = jnp.concatenate(
                            [t[i], t[3][2 * i:2 * i + 2]], axis=0
                        )

    each(nz, send, obs_args)
    each(ns, send, row_args)

    @pl.when(h == 0)
    def _():
        one = jnp.ones((2, 24, 128), F32)
        zero = jnp.zeros((2, 24, 128), F32)
        for i in range(2):
            ast[i, 0] = one
            ast[i, 1] = zero
            ast[i, 2] = zero
            ast[i, 3] = one
            phi[i] = jnp.zeros((8, 8, 128), F32)

    arrived(prx, rsem.at[0])
    arrived(erx, rsem.at[2])
    arrived(mrx, rsem.at[3])

    last = nz * nk

    def chain_copy(buf, i, r):
        return pltpu.make_async_remote_copy(
            src_ref=buf.at[pl.ds(last, 2)], dst_ref=buf.at[pl.ds(0, 2)],
            send_sem=cs.at[i], recv_sem=r,
            device_id={"plane": nz + z, "slab": s}, device_id_type=MESH,
        )

    @pl.when(h == 1)
    def _():
        arrived(ast.at[pl.ds(0, 2)], rsem.at[4])
        arrived(phi.at[pl.ds(0, 2)], rsem.at[5])

    sta_args = lambda q: (ast.at[pl.ds(nk * q, 2)], sta.at[z], sas.at[q], rsem.at[6], q, s)
    stp_args = lambda q: (phi.at[pl.ds(nk * q, 2)], stp.at[z], sps.at[q], rsem.at[7], q, s)

    @pl.loop(0, nz)
    def _(zz):
        for k in range(nk):
            kk = zz * nk + k
            mix = jnp.broadcast_to(mrx[zz, k:k + 1, :], (8, 128))
            wgt = jnp.broadcast_to(mrx[zz, 8 + k:9 + k, :], (8, 128))
            keep = 1.0 - mix
            mix3 = jnp.concatenate([mix] * 3, axis=0)
            wgt3 = jnp.concatenate([wgt] * 3, axis=0)
            keep3 = 1.0 - mix3
            left = jnp.broadcast_to(erx[zz, 0][:, k:k + 1], (8, 128))
            right = jnp.broadcast_to(erx[zz, 1][:, k:k + 1], (8, 128))
            tiles = [prx[zz, i // 2, k, :, pl.ds(128 * (i % 2), 128)] for i in range(8)]
            lefts, rights = neighbours(tiles, left, right, lane)
            for i in range(8):
                phi[kk + 2, i] = mix * phi[kk + 1, i] + keep * phi[kk, i] - wgt * tiles[i]
            for hb in range(2):
                b = [bends(tiles[i], lefts[i], rights[i]) for i in range(4 * hb, 4 * hb + 4)]
                d1 = mix3 - wgt3 * pack4([x[0] for x in b], sub)
                d2 = mix3 - wgt3 * pack4([x[1] for x in b], sub)
                off = -wgt3 * pack4([x[2] for x in b], sub)
                mst[kk, 0, hb] = d1
                mst[kk, 1, hb] = d2
                mst[kk, 2, hb] = off
                now = [ast[kk + 1, c, hb] for c in range(4)]
                before = [ast[kk, c, hb] for c in range(4)]
                new = step_forward(now, before, d1, d2, off, keep3)
                for c in range(4):
                    ast[kk + 2, c, hb] = new[c]
        send(*sta_args(zz))
        send(*stp_args(zz))

    @pl.when(h == 0)
    def _():
        chain_copy(ast, 0, rsem.at[4]).start()
        chain_copy(phi, 1, rsem.at[5]).start()

    def back_copy():
        return pltpu.make_async_remote_copy(
            src_ref=pq.at[0], dst_ref=pq.at[1], send_sem=cs.at[2], recv_sem=rsem.at[8],
            device_id={"plane": z, "slab": s}, device_id_type=MESH,
        )

    @pl.when(h == 1)
    def _():
        pq[0] = jnp.zeros(pq.shape[1:], F32)

    for d in range(nz):
        arrived(orx.at[d], osem.at[d])

    @pl.when(h == 0)
    def _():
        arrived(pq.at[1], rsem.at[8])
        pq[0] = pq[1]

    g_args = lambda zz, j: (
        gsend.at[zz, j], gmid.at[z, j], gs.at[zz, j], gsem.at[z, j], zz, s
    )
    ge_args = lambda zz: (gesend.at[zz], gemid.at[z], ges.at[zz], gesem.at[z], zz, s)

    f_args = lambda c, j: (
        gmid.at[c, j], grx.at[s], fs.at[c, j], rsem.at[9], z, c * per + j
    )
    fl_args = lambda c: (
        gemid.at[c, 0], gerx.at[s], fes.at[c, 0], rsem.at[10], z, (c * per + ns - 1) % ns
    )
    fr_args = lambda c: (
        gemid.at[c, 1], gerx.at[s], fes.at[c, 1], rsem.at[10], z, (c * per + per) % ns
    )

    zero8 = jnp.zeros((8, 128), F32)
    inner = (sub >= 1) & (sub <= 6)

    @pl.loop(0, nz)
    def _(back):
        zz = nz - 1 - back
        el = zero8
        er = zero8
        for k in reversed(range(nk)):
            kk = zz * nk + k
            mix = jnp.broadcast_to(mrx[zz, k:k + 1, :], (24, 128))
            wgt = jnp.broadcast_to(mrx[zz, 8 + k:9 + k, :], (24, 128))
            keep = 1.0 - mix
            c0, c1, c2 = [], [], []
            for hb in range(2):
                nxt = [ast[kk + 2, c, hb] for c in range(4)]
                a = [ast[kk + 1, c, hb] for c in range(4)]
                nw = orx[zz, k, 3, hb]
                r = [nw * (m - orx[zz, k, c, hb]) for c, m in enumerate(shear_of(nxt))]
                tilt = -0.5 * r[2]
                f = [
                    pq[0, 0, hb] - 0.5 * (r[0] + r[1]),
                    pq[0, 1, hb] + tilt,
                    pq[0, 2, hb] + tilt,
                    pq[0, 3, hb] - 0.5 * (r[0] - r[1]),
                ]
                d1, d2, off = mst[kk, 0, hb], mst[kk, 1, hb], mst[kk, 2, hb]
                pq[0, 0, hb] = d1 * f[0] + off * f[2] + pq[0, 4, hb]
                pq[0, 1, hb] = d1 * f[1] + off * f[3] + pq[0, 5, hb]
                pq[0, 2, hb] = off * f[0] + d2 * f[2] + pq[0, 6, hb]
                pq[0, 3, hb] = off * f[1] + d2 * f[3] + pq[0, 7, hb]
                for c in range(4):
                    pq[0, 4 + c, hb] = keep * f[c]
                nwt = -wgt
                c0 += unpack4(nwt * (f[0] * a[0] + f[1] * a[1]), sub)
                c1 += unpack4(nwt * (f[2] * a[2] + f[3] * a[3]), sub)
                c2 += unpack4(nwt * (f[0] * a[2] + f[1] * a[3] + f[2] * a[0] + f[3] * a[1]), sub)
            c0 = [jnp.where(inner, rows_of(t, -1), 0.0) for t in c0]
            c1 = [jnp.where(inner, rows_of(t, -1), 0.0) for t in c1]
            c2 = [jnp.where(inner, rows_of(t, -1), 0.0) for t in c2]
            l1, r1 = neighbours(c1, zero8, zero8, lane)
            l2, r2 = neighbours(c2, zero8, zero8, lane)
            for i in range(8):
                q = 0.25 * (r2[i] - l2[i])
                g = (
                    rows_of(c0[i], 1) - 2.0 * c0[i] + rows_of(c0[i], -1)
                    + (r1[i] - 2.0 * c1[i] + l1[i])
                    + (rows_of(q, 1) - rows_of(q, -1))
                )
                gsend[zz, i // 2, k, :, pl.ds(128 * (i % 2), 128)] = g
            vl = c1[0] + 0.25 * (rows_of(c2[0], 1) - rows_of(c2[0], -1))
            vr = c1[7] - 0.25 * (rows_of(c2[7], 1) - rows_of(c2[7], -1))
            el = jnp.where(lane == k, jnp.broadcast_to(vl[:, 0:1], (8, 128)), el)
            er = jnp.where(lane == k, jnp.broadcast_to(vr[:, 127:128], (8, 128)), er)
        gesend[zz, 0] = el
        gesend[zz, 1] = er
        for j in range(per):
            send(*g_args(zz, j))
        send(*ge_args(zz))

    @pl.when(h == 1)
    def _():
        back_copy().start()

    arrived(prow, rsem.at[1])
    arrived(sta, rsem.at[6])
    arrived(stp, rsem.at[7])
    nchunk = 2 * nz

    @pl.loop(0, nchunk)
    def _(m):
        @pl.when(m % 2 == 0)
        def _():
            away = m // 2
            src = (z + jnp.where(away == 2, 3, jnp.where(away == 3, 2, away))) % nz
            for j in range(per):
                arrived(gmid.at[src, j], gsem.at[src, j])
                send(*f_args(src, j))
            arrived(gemid.at[src], gesem.at[src])
            send(*fl_args(src))
            send(*fr_args(src))

        c = m // 2
        hb = m % 2
        cp = ((m + nchunk - 1) % nchunk) // 2
        cn = ((m + 1) % nchunk) // 2
        tp = (4 * hb + 7) % 8
        tn = (4 * hb + 4) % 8
        y = []
        for b in range(2):
            t = [stp[c, b, 4 * hb + i] for i in range(4)]
            lf, rt = neighbours(
                t, cols_of(stp[cp, b, tp], -1), cols_of(stp[cn, b, tn], 1), lane
            )
            y.append([slopes(t[i], lf[i], rt[i]) for i in range(4)])
        ybefore, ynow = y
        before = [sta[c, 0, e, hb] for e in range(4)]
        now = [sta[c, 1, e, hb] for e in range(4)]
        for k in range(nk):
            mix = mix_in[k]
            wgt = wgt_in[k]
            keep = 1.0 - mix
            t = [
                prow[2 * m + i // 2, k, :, pl.ds(128 * (i % 2), 128)] for i in range(4)
            ]
            left = cols_of(prow[(2 * m + ns - 1) % ns, k, :, pl.ds(128, 128)], -1)
            right = cols_of(prow[(2 * m + 2) % ns, k, :, pl.ds(0, 128)], 1)
            lf, rt = neighbours(t, left, right, lane)
            b = [bends(t[i], lf[i], rt[i]) for i in range(4)]
            d1 = mix - wgt * pack4([x[0] for x in b], sub)
            d2 = mix - wgt * pack4([x[1] for x in b], sub)
            off = -wgt * pack4([x[2] for x in b], sub)
            new = step_forward(now, before, d1, d2, off, keep)
            before, now = now, new
            for e, x in enumerate(shear_of(new)):
                for i, part in enumerate(unpack4(x, sub)):
                    col = pl.ds(pl.multiple_of(m * 512 + i * 128, 128), 128)
                    sv[k, e, :, col] = part[0:6]
            ynew = []
            for i in range(4):
                sl = slopes(t[i], lf[i], rt[i])
                both = []
                for e in range(2):
                    v = mix * ynow[i][e] + keep * ybefore[i][e] - wgt * sl[e]
                    both.append(v)
                    col = pl.ds(pl.multiple_of(m * 512 + i * 128, 128), 128)
                    dv[k, :, e, col] = v[0:6]
                ynew.append(both)
            ybefore, ynow = ynow, ynew

    out_s = pltpu.make_async_copy(sv, shear, lsem.at[3])
    out_d = pltpu.make_async_copy(dv, defl, lsem.at[4])
    out_s.start()
    out_d.start()

    arrived(grx, rsem.at[9])

    @pl.when(on_edge)
    def _():
        arrived(gerx, rsem.at[10])

    @pl.when(pos == 0)
    def _():
        for d in range(ns):
            for k in range(nk):
                e = jnp.broadcast_to(gerx[d][:, k:k + 1], (8, 128))
                grx[d, k, :, 0:128] = grx[d, k, :, 0:128] + jnp.where(lane == 0, e, 0.0)

    @pl.when(pos == per - 1)
    def _():
        for d in range(ns):
            for k in range(nk):
                e = jnp.broadcast_to(gerx[d][:, k:k + 1], (8, 128))
                grx[d, k, :, 128:256] = grx[d, k, :, 128:256] + jnp.where(lane == 127, e, 0.0)

    for d in range(ns):
        for k in range(nk):
            for t in range(2):
                col = pl.ds(128 * t, 128)
                g = grx[d, k, :, col]
                g = g + jnp.where(sub == 1, rows_of(grx[(d + ns - 1) % ns, k, :, col], 6), 0.0)
                g = g + jnp.where(sub == 6, rows_of(grx[(d + 1) % ns, k, :, col], -6), 0.0)
                gv[k, 6 * d:6 * d + 6, col] = rows_of(g, 1)[0:6]
    out_g = pltpu.make_async_copy(gv, grad, lsem.at[5])
    out_g.start()

    each(ns, sent, pix_args)
    each(ns, sent, row_args)

    @pl.when(on_edge)
    def _():
        each(ns, sent, edge_args)

    each(nz, sent, meta_args)
    each(nz, sent, obs_args)
    each(nz, sent, sta_args)
    each(nz, sent, stp_args)

    @pl.when(h == 0)
    def _():
        chain_copy(ast, 0, rsem.at[4]).wait_send()
        chain_copy(phi, 1, rsem.at[5]).wait_send()

    @pl.when(h == 1)
    def _():
        back_copy().wait_send()

    @pl.loop(0, nz)
    def _(zz):
        for j in range(per):
            sent(*g_args(zz, j))
            sent(*f_args(zz, j))
        sent(*ge_args(zz))
        sent(*fl_args(zz))
        sent(*fr_args(zz))

    out_s.wait()
    out_d.wait()
    out_g.wait()


def on_device(nz, ns, potential, mixing, lens_weight, observed, noise_weight):
    nk, total, width = potential.shape
    rows = total // ns
    wide = ns * width
    per = ns // nz
    last = nz * nk
    anyspec = pl.BlockSpec(memory_space=pl.ANY)
    smem = pl.BlockSpec(memory_space=pltpu.SMEM)
    v = lambda *shape: pltpu.VMEM(shape, F32)
    dma = lambda *shape: pltpu.SemaphoreType.DMA(shape)
    defl, shear, grad = pl.pallas_call(
        functools.partial(kernel, nz, ns, nk),
        out_shape=(
            jax.ShapeDtypeStruct((nk, rows, 2, wide), F32),
            jax.ShapeDtypeStruct((nk, 3, rows, wide), F32),
            jax.ShapeDtypeStruct((nk, total, width), F32),
        ),
        in_specs=[anyspec, smem, smem, anyspec, anyspec],
        out_specs=(anyspec, anyspec, anyspec),
        scratch_shapes=[
            v(nk, total, width), v(nk, 3, rows, wide), v(nk, rows, wide),
            v(ns, nk, 8, width), v(ns, 8, 128), v(16, 128), v(nz, nk, 4, 2, 24, 128),
            v(nz, per, nk, 8, width), v(nz, 2, 8, 128), v(nz, 16, 128),
            v(ns, nk, 8, width), v(nz, nk, 4, 2, 24, 128),
            v(last + 2, 4, 2, 24, 128), v(last, 3, 2, 24, 128), v(last + 2, 8, 8, 128),
            v(nz, 2, 4, 2, 24, 128), v(nz, 2, 8, 8, 128), v(2, 8, 2, 24, 128),
            v(nz, per, nk, 8, width), v(nz, 2, 8, 128),
            v(nz, per, nk, 8, width), v(nz, 2, 8, 128), v(ns, nk, 8, width), v(ns, 8, 128),
            v(nk, rows, 2, wide), v(nk, 3, rows, wide), v(nk, total, width),
            dma(6), dma(2, ns), dma(ns), dma(nz), dma(nz), dma(1), dma(nz), dma(nz), dma(3),
            dma(nz, per), dma(nz), dma(nz, per), dma(nz, 2), dma(11), dma(nz), dma(nz, per), dma(nz),
        ],
        name="lens",
        compiler_params=pltpu.CompilerParams(
            collective_id=0, has_side_effects=True, vmem_limit_bytes=60 * 1024 * 1024
        ),
    )(potential, mixing, lens_weight, observed, noise_weight)
    return jnp.transpose(defl, (0, 2, 1, 3)), shear, grad


def solution(mesh):
    nz = mesh.shape["plane"] // NH
    ns = mesh.shape["slab"]
    placed = (
        P("plane", None, "slab"),
        P("plane"),
        P("plane"),
        P("plane", None, "slab", None),
        P("plane", "slab", None),
    )
    return jax.shard_map(
        functools.partial(on_device, nz, ns),
        mesh=mesh,
        in_specs=placed,
        out_specs=(
            P("plane", None, "slab", None),
            P("plane", None, "slab", None),
            P("plane", None, "slab"),
        ),
        check_vma=False,
    )
```

```python
import functools

import jax
import jax.numpy as jnp
from jax import lax
from jax.experimental import pallas as pl
from jax.experimental.pallas import tpu as pltpu
from jax.sharding import PartitionSpec as P

F32 = jnp.float32
MESH = pl.DeviceIdType.MESH
NH = 2


def rows_of(x, shift):
    return pltpu.roll(x, (-shift) % 8, axis=0)


def cols_of(x, shift):
    return pltpu.roll(x, (-shift) % 128, axis=1)


def iotas():
    return (
        lax.broadcasted_iota(jnp.int32, (8, 128), 0),
        lax.broadcasted_iota(jnp.int32, (8, 128), 1),
    )


def pack4(tiles, sub):
    a, b, c, d = tiles
    return jnp.concatenate(
        [
            jnp.where(sub < 6, a, rows_of(d, -6)),
            jnp.where(sub < 6, b, rows_of(d, -4)),
            jnp.where(sub < 6, c, rows_of(d, -2)),
        ],
        axis=0,
    )


def unpack4(x, sub):
    a, b, c = x[0:8], x[8:16], x[16:24]
    d = jnp.where(
        sub < 2, rows_of(a, -2), jnp.where(sub < 4, rows_of(b, -4), rows_of(c, -6))
    )
    return [a, b, c, d]


def neighbours(tiles, left, right, lane):
    ahead = [cols_of(t, -1) for t in tiles]
    behind = [cols_of(t, 1) for t in tiles]
    n = len(tiles)
    lefts = [jnp.where(lane == 0, left if i == 0 else ahead[i - 1], ahead[i]) for i in range(n)]
    rights = [
        jnp.where(lane == 127, right if i == n - 1 else behind[i + 1], behind[i]) for i in range(n)
    ]
    return lefts, rights


def bends(t, lf, rt):
    mid = rows_of(t, 1)
    down = rows_of(t, 2)
    rr = down - 2.0 * mid + t
    cc = rows_of(rt - 2.0 * t + lf, 1)
    q = 0.25 * (rt - lf)
    return rr, cc, rows_of(q, 2) - q


def slopes(t, lf, rt):
    return 0.5 * (rows_of(t, 2) - t), rows_of(0.5 * (rt - lf), 1)


def step_forward(now, before, d1, d2, off, keep):
    return [
        d1 * now[0] + off * now[2] + keep * before[0],
        d1 * now[1] + off * now[3] + keep * before[1],
        off * now[0] + d2 * now[2] + keep * before[2],
        off * now[1] + d2 * now[3] + keep * before[3],
    ]


def shear_of(a):
    return [1.0 - 0.5 * (a[0] + a[3]), 0.5 * (a[3] - a[0]), -0.5 * (a[1] + a[2])]


def exchange(
    nz, ns, nk,
    pot, mix_hbm, wgt_hbm, obs, noi,
    prow, sta, stp, grx, gerx, msend,
    mix_in, wgt_in, pv, ov, nv, psend, esend, osend,
    prx, erx, mrx, orx,
    ast, mst, phi, pq,
    gsend, gmid,
    lsem, ps, es, ms, os_, sas, sps, cs, gs, fs, fes, rsem, osem, gsem, bsem,
):
    h = lax.axis_index("plane") // nz
    z = lax.axis_index("plane") % nz
    s = lax.axis_index("slab")
    per = ns // nz
    blk = s // per
    pos = s % per
    sub, lane = iotas()

    load_p = pltpu.make_async_copy(pot, pv, lsem.at[0])
    load_o = pltpu.make_async_copy(obs, ov, lsem.at[1])
    load_n = pltpu.make_async_copy(noi, nv, lsem.at[2])
    load_m = pltpu.make_async_copy(mix_hbm, mix_in, lsem.at[3])
    load_w = pltpu.make_async_copy(wgt_hbm, wgt_in, lsem.at[4])
    load_p.start()
    load_m.start()
    load_w.start()
    load_o.start()
    load_n.start()

    barrier = pltpu.get_barrier_semaphore()

    @pl.loop(0, nz * ns)
    def _(i):
        zz = i // ns
        ss = i % ns

        @pl.when((zz != z) | (ss != s))
        def _():
            pl.semaphore_signal(
                barrier, inc=1, device_id={"plane": h * nz + zz, "slab": ss}, device_id_type=MESH
            )

    pl.semaphore_signal(
        barrier, inc=1, device_id={"plane": (1 - h) * nz + z, "slab": s}, device_id_type=MESH
    )

    def remote(src, dst, ssem, r, zz, ss):
        return pltpu.make_async_remote_copy(
            src_ref=src, dst_ref=dst, send_sem=ssem, recv_sem=r,
            device_id={"plane": h * nz + zz, "slab": ss}, device_id_type=MESH,
        )

    def send(src, dst, ssem, r, zz, ss):
        own = (zz == z) & (ss == s)

        @pl.when(jnp.logical_not(own))
        def _():
            remote(src, dst, ssem, r, zz, ss).start()

        @pl.when(own)
        def _():
            pltpu.make_async_copy(src, dst, r).start()

    def sent(src, dst, ssem, r, zz, ss):
        @pl.when((zz != z) | (ss != s))
        def _():
            remote(src, dst, ssem, r, zz, ss).wait_send()

    def arrived(buf, r):
        pltpu.make_async_copy(buf, buf, r).wait()

    load_p.wait()
    total = 6 * ns
    for d in range(ns):
        edge = jnp.zeros((8, 128), F32)
        for k in range(nk):
            for t in range(2):
                cols = pl.ds(128 * t, 128)
                if d == 0:
                    v = jnp.where(
                        sub == 0, pv[k, total - 8:total, cols][7:8], rows_of(pv[k, 0:8, cols], -1)
                    )
                elif d == ns - 1:
                    v = jnp.where(
                        sub == 7, pv[k, 0:8, cols][0:1], rows_of(pv[k, total - 8:total, cols], 1)
                    )
                else:
                    v = pv[k, 6 * d - 1:6 * d + 7, cols]
                psend[d, k, :, cols] = v
                if t == 0:
                    first = jnp.broadcast_to(v[:, 0:1], (8, 128))
                else:
                    last = jnp.broadcast_to(v[:, 127:128], (8, 128))
            edge = jnp.where(lane == k, jnp.where(pos == 0, first, last), edge)
        esend[d] = edge
    load_m.wait()
    load_w.wait()
    for k in range(nk):
        msend[k:k + 1, :] = jnp.full((1, 128), mix_in[k], F32)
        msend[8 + k:9 + k, :] = jnp.full((1, 128), wgt_in[k], F32)

    pl.semaphore_wait(barrier, nz * ns)

    eblk = jnp.where(pos == 0, (blk + nz - 1) % nz, (blk + 1) % nz)
    eside = jnp.where(pos == 0, 1, 0)
    on_edge = (pos == 0) | (pos == per - 1)

    def each(n, fn, args):
        @pl.loop(0, n)
        def _(i):
            fn(*args(i))

    pix_args = lambda d: (psend.at[d], prx.at[z, pos], ps.at[0, d], rsem.at[0], blk, d)
    row_args = lambda d: (psend.at[d], prow.at[s], ps.at[1, d], rsem.at[1], z, d)
    edge_args = lambda d: (esend.at[d], erx.at[z, eside], es.at[d], rsem.at[2], eblk, d)
    meta_args = lambda d: (msend, mrx.at[z], ms.at[d], rsem.at[3], d, s)
    obs_args = lambda hb: lambda d: (
        osend.at[hb, d], orx.at[hb, z], os_.at[hb, d], osem.at[hb, z], d, s
    )

    each(ns, send, pix_args)

    @pl.when(on_edge)
    def _():
        each(ns, send, edge_args)

    each(nz, send, meta_args)

    load_o.wait()
    load_n.wait()

    for hb in range(2):

        @pl.loop(0, nz)
        def _(d):
            for k in range(nk):
                for a in range(4):
                    t = []
                    for i in range(4):
                        c = pl.ds(pl.multiple_of(d * 1024 + (hb * 4 + i) * 128, 128), 128)
                        t.append(ov[k, a, :, c] if a < 3 else nv[k, :, c])
                    for i in range(3):
                        osend[hb, d, k, a, pl.ds(8 * i, 8), :] = jnp.concatenate(
                            [t[i], t[3][2 * i:2 * i + 2]], axis=0
                        )

        each(nz, send, obs_args(hb))

    each(ns, send, row_args)

    @pl.when(h == 0)
    def _():
        one = jnp.ones((2, 24, 128), F32)
        zero = jnp.zeros((2, 24, 128), F32)
        for i in range(2):
            ast[i, 0] = one
            ast[i, 1] = zero
            ast[i, 2] = zero
            ast[i, 3] = one
            phi[i] = jnp.zeros((8, 8, 128), F32)

    arrived(prx, rsem.at[0])
    arrived(erx, rsem.at[2])
    arrived(mrx, rsem.at[3])

    last = nz * nk

    def chain_copy(buf, i, r):
        return pltpu.make_async_remote_copy(
            src_ref=buf.at[pl.ds(last, 2)], dst_ref=buf.at[pl.ds(0, 2)],
            send_sem=cs.at[i], recv_sem=r,
            device_id={"plane": nz + z, "slab": s}, device_id_type=MESH,
        )

    @pl.when(h == 1)
    def _():
        arrived(ast.at[pl.ds(0, 2)], rsem.at[4])
        arrived(phi.at[pl.ds(0, 2)], rsem.at[5])

    sta_args = lambda q: (ast.at[pl.ds(nk * q, 2)], sta.at[z], sas.at[q], rsem.at[6], q, s)
    stp_args = lambda q: (phi.at[pl.ds(nk * q, 2)], stp.at[z], sps.at[q], rsem.at[7], q, s)

    @pl.loop(0, nz)
    def _(zz):
        for k in range(nk):
            kk = zz * nk + k
            mix = jnp.broadcast_to(mrx[zz, k:k + 1, :], (8, 128))
            wgt = jnp.broadcast_to(mrx[zz, 8 + k:9 + k, :], (8, 128))
            keep = 1.0 - mix
            mix3 = jnp.concatenate([mix] * 3, axis=0)
            wgt3 = jnp.concatenate([wgt] * 3, axis=0)
            keep3 = 1.0 - mix3
            left = jnp.broadcast_to(erx[zz, 0][:, k:k + 1], (8, 128))
            right = jnp.broadcast_to(erx[zz, 1][:, k:k + 1], (8, 128))
            tiles = [prx[zz, i // 2, k, :, pl.ds(128 * (i % 2), 128)] for i in range(8)]
            lefts, rights = neighbours(tiles, left, right, lane)
            for i in range(8):
                phi[kk + 2, i] = mix * phi[kk + 1, i] + keep * phi[kk, i] - wgt * tiles[i]
            for hb in range(2):
                b = [bends(tiles[i], lefts[i], rights[i]) for i in range(4 * hb, 4 * hb + 4)]
                d1 = mix3 - wgt3 * pack4([x[0] for x in b], sub)
                d2 = mix3 - wgt3 * pack4([x[1] for x in b], sub)
                off = -wgt3 * pack4([x[2] for x in b], sub)
                mst[kk, 0, hb] = d1
                mst[kk, 1, hb] = d2
                mst[kk, 2, hb] = off
                now = [ast[kk + 1, c, hb] for c in range(4)]
                before = [ast[kk, c, hb] for c in range(4)]
                new = step_forward(now, before, d1, d2, off, keep3)
                for c in range(4):
                    ast[kk + 2, c, hb] = new[c]
        @pl.when((h == 0) & (zz > 0))
        def _():
            send(*sta_args(zz))
            send(*stp_args(zz))

    @pl.when((h == 0) & (z == 0))
    def _():
        for c in range(nz):
            pltpu.make_async_copy(ast.at[pl.ds(0, 2)], sta.at[c], rsem.at[6]).start()
            pltpu.make_async_copy(phi.at[pl.ds(0, 2)], stp.at[c], rsem.at[7]).start()

    @pl.when(h == 0)
    def _():
        chain_copy(ast, 0, rsem.at[4]).start()
        chain_copy(phi, 1, rsem.at[5]).start()

    def back_copy(hb):
        return pltpu.make_async_remote_copy(
            src_ref=pq.at[hb], dst_ref=pq.at[hb], send_sem=cs.at[2 + hb], recv_sem=bsem.at[hb],
            device_id={"plane": z, "slab": s}, device_id_type=MESH,
        )

    @pl.when(h == 1)
    def _():
        pq[...] = jnp.zeros(pq.shape, F32)

    g_args = lambda hb, zz: (
        gsend.at[hb, zz], gmid.at[hb, z], gs.at[hb, zz], gsem.at[hb, z], zz, s
    )
    tiles_of = 2 * nk

    f_args = lambda hb, c, j: (
        gmid.at[hb, c, pl.ds(j * tiles_of, tiles_of)], grx.at[s], fs.at[hb, c, j], rsem.at[9],
        z, c * per + hb * 2 + j,
    )
    fe_args = lambda hb, c, e: (
        gmid.at[hb, c, 2 * tiles_of + e], gerx.at[s], fes.at[hb, c, e], rsem.at[10],
        z, (c * per + hb * 2 + (2 if e else ns - 1)) % ns,
    )

    zero8 = jnp.zeros((8, 128), F32)
    inner = (sub >= 1) & (sub <= 6)

    for hb in range(2):
        for d in range(nz):
            arrived(orx.at[hb, d], osem.at[hb, d])

        @pl.when(h == 0)
        def _():
            arrived(pq.at[hb], bsem.at[hb])

        @pl.loop(0, nz)
        def _(back):
            zz = nz - 1 - back
            el = zero8
            er = zero8
            for k in reversed(range(nk)):
                kk = zz * nk + k
                mix = jnp.broadcast_to(mrx[zz, k:k + 1, :], (24, 128))
                nwt = -jnp.broadcast_to(mrx[zz, 8 + k:9 + k, :], (24, 128))
                keep = 1.0 - mix
                nxt = [ast[kk + 2, c, hb] for c in range(4)]
                a = [ast[kk + 1, c, hb] for c in range(4)]
                nw = orx[hb, zz, k, 3]
                r = [nw * (m - orx[hb, zz, k, c]) for c, m in enumerate(shear_of(nxt))]
                tilt = -0.5 * r[2]
                f = [
                    pq[hb, 0] - 0.5 * (r[0] + r[1]),
                    pq[hb, 1] + tilt,
                    pq[hb, 2] + tilt,
                    pq[hb, 3] - 0.5 * (r[0] - r[1]),
                ]
                d1, d2, off = mst[kk, 0, hb], mst[kk, 1, hb], mst[kk, 2, hb]
                pq[hb, 0] = d1 * f[0] + off * f[2] + pq[hb, 4]
                pq[hb, 1] = d1 * f[1] + off * f[3] + pq[hb, 5]
                pq[hb, 2] = off * f[0] + d2 * f[2] + pq[hb, 6]
                pq[hb, 3] = off * f[1] + d2 * f[3] + pq[hb, 7]
                for c in range(4):
                    pq[hb, 4 + c] = keep * f[c]
                c0 = unpack4(nwt * (f[0] * a[0] + f[1] * a[1]), sub)
                c1 = unpack4(nwt * (f[2] * a[2] + f[3] * a[3]), sub)
                c2 = unpack4(nwt * (f[0] * a[2] + f[1] * a[3] + f[2] * a[0] + f[3] * a[1]), sub)
                c0 = [jnp.where(inner, rows_of(t, -1), 0.0) for t in c0]
                c1 = [jnp.where(inner, rows_of(t, -1), 0.0) for t in c1]
                c2 = [jnp.where(inner, rows_of(t, -1), 0.0) for t in c2]
                l1, r1 = neighbours(c1, zero8, zero8, lane)
                l2, r2 = neighbours(c2, zero8, zero8, lane)
                for i in range(4):
                    q = 0.25 * (r2[i] - l2[i])
                    gsend[hb, zz, (i // 2) * tiles_of + 2 * k + i % 2] = (
                        rows_of(c0[i], 1) - 2.0 * c0[i] + rows_of(c0[i], -1)
                        + (r1[i] - 2.0 * c1[i] + l1[i])
                        + (rows_of(q, 1) - rows_of(q, -1))
                    )
                vl = c1[0] + 0.25 * (rows_of(c2[0], 1) - rows_of(c2[0], -1))
                vr = c1[3] - 0.25 * (rows_of(c2[3], 1) - rows_of(c2[3], -1))
                el = jnp.where(lane == k, jnp.broadcast_to(vl[:, 0:1], (8, 128)), el)
                er = jnp.where(lane == k, jnp.broadcast_to(vr[:, 127:128], (8, 128)), er)
            gsend[hb, zz, 2 * tiles_of] = el
            gsend[hb, zz, 2 * tiles_of + 1] = er
            send(*g_args(hb, zz))

        @pl.when(h == 1)
        def _():
            back_copy(hb).start()

    @pl.when(h == 1)
    def _():
        @pl.loop(0, nz)
        def _(zz):
            send(*sta_args(zz))
            send(*stp_args(zz))

    for hb in range(2):

        @pl.loop(0, nz)
        def _(away):
            c = (z + jnp.where(away == 2, 3, jnp.where(away == 3, 2, away))) % nz
            arrived(gmid.at[hb, c], gsem.at[hb, c])
            for j in range(2):
                send(*f_args(hb, c, j))
                send(*fe_args(hb, c, j))

    arrived(prow, rsem.at[1])
    arrived(grx, rsem.at[9])
    arrived(gerx, rsem.at[10])
    arrived(sta, rsem.at[6])
    arrived(stp, rsem.at[7])

    each(ns, sent, pix_args)
    each(ns, sent, row_args)

    @pl.when(on_edge)
    def _():
        each(ns, sent, edge_args)

    each(nz, sent, meta_args)
    for hb in range(2):
        each(nz, sent, obs_args(hb))

    @pl.loop(0, nz)
    def _(zz):
        @pl.when((h == 1) | (zz > 0))
        def _():
            sent(*sta_args(zz))
            sent(*stp_args(zz))

        for hb in range(2):
            sent(*g_args(hb, zz))
            for j in range(2):
                sent(*f_args(hb, zz, j))
                sent(*fe_args(hb, zz, j))

    @pl.when(h == 0)
    def _():
        chain_copy(ast, 0, rsem.at[4]).wait_send()
        chain_copy(phi, 1, rsem.at[5]).wait_send()

    @pl.when(h == 1)
    def _():
        back_copy(0).wait_send()
        back_copy(1).wait_send()


def finish(
    nz, ns, nk,
    prow, sta, stp, grx, gerx, meta,
    defl, shear, grad,
    dv, sv, gv, ssem, dsem, gsem,
):
    sub, lane = iotas()
    nchunk = 2 * nz
    odd = lax.axis_index("slab") % 2

    def out_s(m):
        col = pl.ds(pl.multiple_of(m * 512, 512), 512)
        return pltpu.make_async_copy(sv.at[:, :, :, col], shear.at[:, :, :, col], ssem.at[m])

    def out_d(m):
        col = pl.ds(pl.multiple_of(m * 512, 512), 512)
        return pltpu.make_async_copy(dv.at[:, :, :, col], defl.at[:, :, :, col], dsem.at[m])

    @pl.loop(0, nchunk)
    def _(m):
        c = m // 2
        hb = m % 2
        cp = ((m + nchunk - 1) % nchunk) // 2
        cn = ((m + 1) % nchunk) // 2
        tp = (4 * hb + 7) % 8
        tn = (4 * hb + 4) % 8
        y = []
        for b in range(2):
            t = [stp[c, b, 4 * hb + i] for i in range(4)]
            lf, rt = neighbours(
                t, cols_of(stp[cp, b, tp], -1), cols_of(stp[cn, b, tn], 1), lane
            )
            y.append([slopes(t[i], lf[i], rt[i]) for i in range(4)])
        ybefore, ynow = y
        before = [sta[c, 0, e, hb] for e in range(4)]
        now = [sta[c, 1, e, hb] for e in range(4)]
        for k in range(nk):
            mix3 = jnp.broadcast_to(meta[k:k + 1, :], (24, 128))
            wgt3 = jnp.broadcast_to(meta[8 + k:9 + k, :], (24, 128))
            mix, wgt = mix3[0:8], wgt3[0:8]
            keep3 = 1.0 - mix3
            keep = 1.0 - mix
            t = [
                prow[2 * m + i // 2, k, :, pl.ds(128 * (i % 2), 128)] for i in range(4)
            ]
            left = cols_of(prow[(2 * m + ns - 1) % ns, k, :, pl.ds(128, 128)], -1)
            right = cols_of(prow[(2 * m + 2) % ns, k, :, pl.ds(0, 128)], 1)
            lf, rt = neighbours(t, left, right, lane)
            b = [bends(t[i], lf[i], rt[i]) for i in range(4)]
            d1 = mix3 - wgt3 * pack4([x[0] for x in b], sub)
            d2 = mix3 - wgt3 * pack4([x[1] for x in b], sub)
            off = -wgt3 * pack4([x[2] for x in b], sub)
            new = step_forward(now, before, d1, d2, off, keep3)
            before, now = now, new
            for e, x in enumerate(shear_of(new)):
                for i, part in enumerate(unpack4(x, sub)):
                    col = pl.ds(pl.multiple_of(m * 512 + i * 128, 128), 128)
                    sv[k, e, :, col] = part[0:6]
            ynew = []
            for i in range(4):
                sl = slopes(t[i], lf[i], rt[i])
                both = []
                for e in range(2):
                    v = mix * ynow[i][e] + keep * ybefore[i][e] - wgt * sl[e]
                    both.append(v)
                    col = pl.ds(pl.multiple_of(m * 512 + i * 128, 128), 128)
                    dv[k, :, e, col] = v[0:6]
                ynew.append(both)
            ybefore, ynow = ynow, ynew
        out_s(m).start()
        out_d(m).start()

    spot = lane == jnp.where(odd == 1, 127, 0)
    for k in range(nk):
        for t in range(2):
            part = []
            for d in range(ns):
                edge = jnp.broadcast_to(gerx[d][:, k:k + 1], (8, 128))
                part.append(grx[d, 2 * k + t] + jnp.where(spot & (odd == t), edge, 0.0))
            for d in range(ns):
                g = part[d]
                g = g + jnp.where(sub == 1, rows_of(part[(d + ns - 1) % ns], 6), 0.0)
                g = g + jnp.where(sub == 6, rows_of(part[(d + 1) % ns], -6), 0.0)
                gv[k, 6 * d:6 * d + 6, pl.ds(128 * t, 128)] = rows_of(g, 1)[0:6]
    out_g = pltpu.make_async_copy(gv, grad, gsem.at[0])
    out_g.start()

    @pl.loop(0, nchunk)
    def _(m):
        out_s(m).wait()
        out_d(m).wait()

    out_g.wait()


def on_device(nz, ns, potential, mixing, lens_weight, observed, noise_weight):
    nk, total, width = potential.shape
    rows = total // ns
    wide = ns * width
    per = ns // nz
    last = nz * nk
    anyspec = pl.BlockSpec(memory_space=pl.ANY)
    hbm = pl.BlockSpec(memory_space=pltpu.HBM)
    vmem = pl.BlockSpec(memory_space=pltpu.VMEM)
    smem = pl.BlockSpec(memory_space=pltpu.SMEM)
    v = lambda *shape: pltpu.VMEM(shape, F32)
    dma = lambda *shape: pltpu.SemaphoreType.DMA(shape)
    received = [
        (ns, nk, 8, width), (nz, 2, 4, 2, 24, 128), (nz, 2, 8, 8, 128),
        (ns, 2 * nk, 8, 128), (ns, 8, 128), (16, 128),
    ]
    stay = lambda x: pltpu.with_memory_space_constraint(x, pltpu.HBM)
    shaped = lambda shape: jax.ShapeDtypeStruct(shape, F32)
    mids = pl.pallas_call(
        functools.partial(exchange, nz, ns, nk),
        out_shape=tuple(shaped(x) for x in received),
        in_specs=[hbm] * 5,
        out_specs=(vmem,) * 6,
        scratch_shapes=[
            pltpu.SMEM((nk,), F32), pltpu.SMEM((nk,), F32),
            v(nk, total, width), v(nk, 3, rows, wide), v(nk, rows, wide),
            v(ns, nk, 8, width), v(ns, 8, 128), v(2, nz, nk, 4, 24, 128),
            v(nz, per, nk, 8, width), v(nz, 2, 8, 128), v(nz, 16, 128), v(2, nz, nk, 4, 24, 128),
            v(last + 2, 4, 2, 24, 128), v(last, 3, 2, 24, 128), v(last + 2, 8, 8, 128),
            v(2, 8, 24, 128),
            v(2, nz, 4 * nk + 2, 8, 128), v(2, nz, 4 * nk + 2, 8, 128),
            dma(6), dma(2, ns), dma(ns), dma(nz), dma(2, nz), dma(nz), dma(nz), dma(4),
            dma(2, nz), dma(2, nz, 2), dma(2, nz, 2), dma(11), dma(2, nz), dma(2, nz), dma(2),
        ],
        name="exchange",
        compiler_params=pltpu.CompilerParams(
            collective_id=0, has_side_effects=True, vmem_limit_bytes=24 * 1024 * 1024
        ),
    )(stay(potential), stay(mixing), stay(lens_weight), stay(observed), stay(noise_weight))
    defl, shear, grad = pl.pallas_call(
        functools.partial(finish, nz, ns, nk),
        out_shape=(
            shaped((nk, rows, 2, wide)), shaped((nk, 3, rows, wide)), shaped((nk, total, width)),
        ),
        in_specs=[vmem] * 6,
        out_specs=(hbm,) * 3,
        scratch_shapes=[
            v(nk, rows, 2, wide), v(nk, 3, rows, wide), v(nk, total, width),
            dma(2 * nz), dma(2 * nz), dma(1),
        ],
        name="finish",
        compiler_params=pltpu.CompilerParams(vmem_limit_bytes=24 * 1024 * 1024),
    )(*mids)
    return jnp.transpose(defl, (0, 2, 1, 3)), shear, grad


def solution(mesh):
    nz = mesh.shape["plane"] // NH
    ns = mesh.shape["slab"]
    placed = (
        P("plane", None, "slab"),
        P("plane"),
        P("plane"),
        P("plane", None, "slab", None),
        P("plane", "slab", None),
    )
    return jax.shard_map(
        functools.partial(on_device, nz, ns),
        mesh=mesh,
        in_specs=placed,
        out_specs=(
            P("plane", None, "slab", None),
            P("plane", None, "slab", None),
            P("plane", None, "slab"),
        ),
        check_vma=False,
    )
```

```python
import functools

import jax
import jax.numpy as jnp
from jax import lax
from jax.experimental import pallas as pl
from jax.experimental.pallas import tpu as pltpu
from jax.sharding import PartitionSpec as P

F32 = jnp.float32
MESH = pl.DeviceIdType.MESH
NH = 2


def rows_of(x, shift):
    return pltpu.roll(x, (-shift) % 8, axis=0)


def cols_of(x, shift):
    return pltpu.roll(x, (-shift) % 128, axis=1)


def iotas():
    return (
        lax.broadcasted_iota(jnp.int32, (8, 128), 0),
        lax.broadcasted_iota(jnp.int32, (8, 128), 1),
    )


def pack4(tiles, sub):
    a, b, c, d = tiles
    return jnp.concatenate(
        [
            jnp.where(sub < 6, a, rows_of(d, -6)),
            jnp.where(sub < 6, b, rows_of(d, -4)),
            jnp.where(sub < 6, c, rows_of(d, -2)),
        ],
        axis=0,
    )


def unpack4(x, sub):
    a, b, c = x[0:8], x[8:16], x[16:24]
    d = jnp.where(
        sub < 2, rows_of(a, -2), jnp.where(sub < 4, rows_of(b, -4), rows_of(c, -6))
    )
    return [a, b, c, d]


def neighbours(tiles, left, right, lane):
    ahead = [cols_of(t, -1) for t in tiles]
    behind = [cols_of(t, 1) for t in tiles]
    n = len(tiles)
    lefts = [jnp.where(lane == 0, left if i == 0 else ahead[i - 1], ahead[i]) for i in range(n)]
    rights = [
        jnp.where(lane == 127, right if i == n - 1 else behind[i + 1], behind[i]) for i in range(n)
    ]
    return lefts, rights


def bends(t, lf, rt):
    mid = rows_of(t, 1)
    down = rows_of(t, 2)
    rr = down - 2.0 * mid + t
    cc = rows_of(rt - 2.0 * t + lf, 1)
    q = 0.25 * (rt - lf)
    return rr, cc, rows_of(q, 2) - q


def slopes(t, lf, rt):
    return 0.5 * (rows_of(t, 2) - t), rows_of(0.5 * (rt - lf), 1)


def step_forward(now, before, d1, d2, off, keep):
    return [
        d1 * now[0] + off * now[2] + keep * before[0],
        d1 * now[1] + off * now[3] + keep * before[1],
        off * now[0] + d2 * now[2] + keep * before[2],
        off * now[1] + d2 * now[3] + keep * before[3],
    ]


def shear_of(a):
    return [1.0 - 0.5 * (a[0] + a[3]), 0.5 * (a[3] - a[0]), -0.5 * (a[1] + a[2])]


def exchange(
    nz, ns, nk,
    pot, mix_hbm, wgt_hbm, obs, noi,
    dv, sv, grx, gerx,
    mix_in, wgt_in, pv, ov, nv, psend, esend, osend,
    prow, sta, stp, msend,
    prx, erx, mrx, orx,
    ast, mst, phi, pq,
    gsend, gmid,
    lsem, ps, es, ms, os_, sas, sps, cs, gs, fs, fes, rsem, osem, gsem, bsem, stsem,
):
    h = lax.axis_index("plane") // nz
    z = lax.axis_index("plane") % nz
    s = lax.axis_index("slab")
    per = ns // nz
    blk = s // per
    pos = s % per
    sub, lane = iotas()

    load_p = pltpu.make_async_copy(pot, pv, lsem.at[0])
    load_o = pltpu.make_async_copy(obs, ov, lsem.at[1])
    load_n = pltpu.make_async_copy(noi, nv, lsem.at[2])
    load_m = pltpu.make_async_copy(mix_hbm, mix_in, lsem.at[3])
    load_w = pltpu.make_async_copy(wgt_hbm, wgt_in, lsem.at[4])
    load_p.start()
    load_m.start()
    load_w.start()
    load_o.start()
    load_n.start()

    barrier = pltpu.get_barrier_semaphore()

    @pl.loop(0, nz * ns)
    def _(i):
        zz = i // ns
        ss = i % ns

        @pl.when((zz != z) | (ss != s))
        def _():
            pl.semaphore_signal(
                barrier, inc=1, device_id={"plane": h * nz + zz, "slab": ss}, device_id_type=MESH
            )

    pl.semaphore_signal(
        barrier, inc=1, device_id={"plane": (1 - h) * nz + z, "slab": s}, device_id_type=MESH
    )

    def remote(src, dst, ssem, r, zz, ss):
        return pltpu.make_async_remote_copy(
            src_ref=src, dst_ref=dst, send_sem=ssem, recv_sem=r,
            device_id={"plane": h * nz + zz, "slab": ss}, device_id_type=MESH,
        )

    def send(src, dst, ssem, r, zz, ss):
        own = (zz == z) & (ss == s)

        @pl.when(jnp.logical_not(own))
        def _():
            remote(src, dst, ssem, r, zz, ss).start()

        @pl.when(own)
        def _():
            pltpu.make_async_copy(src, dst, r).start()

    def sent(src, dst, ssem, r, zz, ss):
        @pl.when((zz != z) | (ss != s))
        def _():
            remote(src, dst, ssem, r, zz, ss).wait_send()

    def arrived(buf, r):
        pltpu.make_async_copy(buf, buf, r).wait()

    load_p.wait()
    total = 6 * ns
    for d in range(ns):
        edge = jnp.zeros((8, 128), F32)
        for k in range(nk):
            for t in range(2):
                cols = pl.ds(128 * t, 128)
                if d == 0:
                    v = jnp.where(
                        sub == 0, pv[k, total - 8:total, cols][7:8], rows_of(pv[k, 0:8, cols], -1)
                    )
                elif d == ns - 1:
                    v = jnp.where(
                        sub == 7, pv[k, 0:8, cols][0:1], rows_of(pv[k, total - 8:total, cols], 1)
                    )
                else:
                    v = pv[k, 6 * d - 1:6 * d + 7, cols]
                psend[d, k, :, cols] = v
                if t == 0:
                    first = jnp.broadcast_to(v[:, 0:1], (8, 128))
                else:
                    last = jnp.broadcast_to(v[:, 127:128], (8, 128))
            edge = jnp.where(lane == k, jnp.where(pos == 0, first, last), edge)
        esend[d] = edge
    load_m.wait()
    load_w.wait()
    for k in range(nk):
        msend[k:k + 1, :] = jnp.full((1, 128), mix_in[k], F32)
        msend[8 + k:9 + k, :] = jnp.full((1, 128), wgt_in[k], F32)

    pl.semaphore_wait(barrier, nz * ns)

    eblk = jnp.where(pos == 0, (blk + nz - 1) % nz, (blk + 1) % nz)
    eside = jnp.where(pos == 0, 1, 0)
    on_edge = (pos == 0) | (pos == per - 1)

    def each(n, fn, args):
        first = s if n == ns else z

        @pl.loop(0, n)
        def _(i):
            fn(*args((first + i) % n))

    pix_args = lambda d: (psend.at[d], prx.at[z, pos], ps.at[0, d], rsem.at[0], blk, d)
    row_args = lambda d: (psend.at[d], prow.at[s], ps.at[1, d], rsem.at[1], z, d)
    edge_args = lambda d: (esend.at[d], erx.at[z, eside], es.at[d], rsem.at[2], eblk, d)
    meta_args = lambda d: (msend, mrx.at[z], ms.at[d], rsem.at[3], d, s)
    obs_args = lambda hb: lambda d: (
        osend.at[hb, d], orx.at[hb, z], os_.at[hb, d], osem.at[hb, z], d, s
    )

    each(ns, send, pix_args)

    @pl.when(on_edge)
    def _():
        each(ns, send, edge_args)

    each(nz, send, meta_args)

    load_o.wait()
    load_n.wait()

    for hb in range(2):

        @pl.loop(0, nz)
        def _(d):
            for k in range(nk):
                for a in range(4):
                    t = []
                    for i in range(4):
                        c = pl.ds(pl.multiple_of(d * 1024 + (hb * 4 + i) * 128, 128), 128)
                        t.append(ov[k, a, :, c] if a < 3 else nv[k, :, c])
                    for i in range(3):
                        osend[hb, d, k, a, pl.ds(8 * i, 8), :] = jnp.concatenate(
                            [t[i], t[3][2 * i:2 * i + 2]], axis=0
                        )

        each(nz, send, obs_args(hb))

    each(ns, send, row_args)

    @pl.when(h == 0)
    def _():
        one = jnp.ones((2, 24, 128), F32)
        zero = jnp.zeros((2, 24, 128), F32)
        for i in range(2):
            ast[i, 0] = one
            ast[i, 1] = zero
            ast[i, 2] = zero
            ast[i, 3] = one
            phi[i] = jnp.zeros((8, 8, 128), F32)

    arrived(prx, rsem.at[0])
    arrived(erx, rsem.at[2])
    arrived(mrx, rsem.at[3])

    last = nz * nk

    def chain_copy(buf, i, r):
        return pltpu.make_async_remote_copy(
            src_ref=buf.at[pl.ds(last, 2)], dst_ref=buf.at[pl.ds(0, 2)],
            send_sem=cs.at[i], recv_sem=r,
            device_id={"plane": nz + z, "slab": s}, device_id_type=MESH,
        )

    @pl.when(h == 1)
    def _():
        arrived(ast.at[pl.ds(0, 2)], rsem.at[4])
        arrived(phi.at[pl.ds(0, 2)], rsem.at[5])

    sta_args = lambda q: (ast.at[pl.ds(nk * q, 2)], sta.at[z], sas.at[q], stsem.at[z], q, s)
    stp_args = lambda q: (phi.at[pl.ds(nk * q, 2)], stp.at[z], sps.at[q], rsem.at[7], q, s)

    @pl.loop(0, nz)
    def _(zz):
        for k in range(nk):
            kk = zz * nk + k
            mix = jnp.broadcast_to(mrx[zz, k:k + 1, :], (8, 128))
            wgt = jnp.broadcast_to(mrx[zz, 8 + k:9 + k, :], (8, 128))
            keep = 1.0 - mix
            mix3 = jnp.concatenate([mix] * 3, axis=0)
            wgt3 = jnp.concatenate([wgt] * 3, axis=0)
            keep3 = 1.0 - mix3
            left = jnp.broadcast_to(erx[zz, 0][:, k:k + 1], (8, 128))
            right = jnp.broadcast_to(erx[zz, 1][:, k:k + 1], (8, 128))
            tiles = [prx[zz, i // 2, k, :, pl.ds(128 * (i % 2), 128)] for i in range(8)]
            lefts, rights = neighbours(tiles, left, right, lane)
            for i in range(8):
                phi[kk + 2, i] = mix * phi[kk + 1, i] + keep * phi[kk, i] - wgt * tiles[i]
            for hb in range(2):
                b = [bends(tiles[i], lefts[i], rights[i]) for i in range(4 * hb, 4 * hb + 4)]
                d1 = mix3 - wgt3 * pack4([x[0] for x in b], sub)
                d2 = mix3 - wgt3 * pack4([x[1] for x in b], sub)
                off = -wgt3 * pack4([x[2] for x in b], sub)
                mst[kk, 0, hb] = d1
                mst[kk, 1, hb] = d2
                mst[kk, 2, hb] = off
                now = [ast[kk + 1, c, hb] for c in range(4)]
                before = [ast[kk, c, hb] for c in range(4)]
                new = step_forward(now, before, d1, d2, off, keep3)
                for c in range(4):
                    ast[kk + 2, c, hb] = new[c]
        @pl.when((h == 0) & (zz > 0))
        def _():
            send(*sta_args(zz))
            send(*stp_args(zz))

    @pl.when((h == 0) & (z == 0))
    def _():
        for c in range(nz):
            pltpu.make_async_copy(ast.at[pl.ds(0, 2)], sta.at[c], stsem.at[c]).start()
            pltpu.make_async_copy(phi.at[pl.ds(0, 2)], stp.at[c], rsem.at[7]).start()

    @pl.when(h == 0)
    def _():
        chain_copy(ast, 0, rsem.at[4]).start()
        chain_copy(phi, 1, rsem.at[5]).start()

    def near_first(i):
        return (z + jnp.where(i == 2, 3, jnp.where(i == 3, 2, i))) % nz

    def back_copy(hb):
        return pltpu.make_async_remote_copy(
            src_ref=pq.at[hb], dst_ref=pq.at[hb], send_sem=cs.at[2 + hb], recv_sem=bsem.at[hb],
            device_id={"plane": z, "slab": s}, device_id_type=MESH,
        )

    @pl.when(h == 1)
    def _():
        pq[...] = jnp.zeros(pq.shape, F32)

    g_args = lambda hb, zz: (
        gsend.at[hb, zz], gmid.at[hb, z], gs.at[hb, zz], gsem.at[hb, z], zz, s
    )
    tiles_of = 2 * nk

    f_args = lambda hb, c, j: (
        gmid.at[hb, c, pl.ds(j * tiles_of, tiles_of)], grx.at[s], fs.at[hb, c, j], rsem.at[9],
        z, c * per + hb * 2 + j,
    )
    fe_args = lambda hb, c, e: (
        gmid.at[hb, c, 2 * tiles_of + e], gerx.at[s], fes.at[hb, c, e], rsem.at[10],
        z, (c * per + hb * 2 + (2 if e else ns - 1)) % ns,
    )

    zero8 = jnp.zeros((8, 128), F32)
    inner = (sub >= 1) & (sub <= 6)

    for hb in range(2):
        for d in range(nz):
            arrived(orx.at[hb, d], osem.at[hb, d])

        @pl.when(h == 0)
        def _():
            arrived(pq.at[hb], bsem.at[hb])

        @pl.loop(0, nz)
        def _(back):
            zz = nz - 1 - back
            el = zero8
            er = zero8
            for k in reversed(range(nk)):
                kk = zz * nk + k
                mix = jnp.broadcast_to(mrx[zz, k:k + 1, :], (24, 128))
                nwt = -jnp.broadcast_to(mrx[zz, 8 + k:9 + k, :], (24, 128))
                keep = 1.0 - mix
                nxt = [ast[kk + 2, c, hb] for c in range(4)]
                a = [ast[kk + 1, c, hb] for c in range(4)]
                nw = orx[hb, zz, k, 3]
                r = [nw * (m - orx[hb, zz, k, c]) for c, m in enumerate(shear_of(nxt))]
                tilt = -0.5 * r[2]
                f = [
                    pq[hb, 0] - 0.5 * (r[0] + r[1]),
                    pq[hb, 1] + tilt,
                    pq[hb, 2] + tilt,
                    pq[hb, 3] - 0.5 * (r[0] - r[1]),
                ]
                d1, d2, off = mst[kk, 0, hb], mst[kk, 1, hb], mst[kk, 2, hb]
                pq[hb, 0] = d1 * f[0] + off * f[2] + pq[hb, 4]
                pq[hb, 1] = d1 * f[1] + off * f[3] + pq[hb, 5]
                pq[hb, 2] = off * f[0] + d2 * f[2] + pq[hb, 6]
                pq[hb, 3] = off * f[1] + d2 * f[3] + pq[hb, 7]
                for c in range(4):
                    pq[hb, 4 + c] = keep * f[c]
                c0 = unpack4(nwt * (f[0] * a[0] + f[1] * a[1]), sub)
                c1 = unpack4(nwt * (f[2] * a[2] + f[3] * a[3]), sub)
                c2 = unpack4(nwt * (f[0] * a[2] + f[1] * a[3] + f[2] * a[0] + f[3] * a[1]), sub)
                c0 = [jnp.where(inner, rows_of(t, -1), 0.0) for t in c0]
                c1 = [jnp.where(inner, rows_of(t, -1), 0.0) for t in c1]
                c2 = [jnp.where(inner, rows_of(t, -1), 0.0) for t in c2]
                l1, r1 = neighbours(c1, zero8, zero8, lane)
                l2, r2 = neighbours(c2, zero8, zero8, lane)
                for i in range(4):
                    q = 0.25 * (r2[i] - l2[i])
                    gsend[hb, zz, (i // 2) * tiles_of + 2 * k + i % 2] = (
                        rows_of(c0[i], 1) - 2.0 * c0[i] + rows_of(c0[i], -1)
                        + (r1[i] - 2.0 * c1[i] + l1[i])
                        + (rows_of(q, 1) - rows_of(q, -1))
                    )
                vl = c1[0] + 0.25 * (rows_of(c2[0], 1) - rows_of(c2[0], -1))
                vr = c1[3] - 0.25 * (rows_of(c2[3], 1) - rows_of(c2[3], -1))
                el = jnp.where(lane == k, jnp.broadcast_to(vl[:, 0:1], (8, 128)), el)
                er = jnp.where(lane == k, jnp.broadcast_to(vr[:, 127:128], (8, 128)), er)
            gsend[hb, zz, 2 * tiles_of] = el
            gsend[hb, zz, 2 * tiles_of + 1] = er
            send(*g_args(hb, zz))

        @pl.when(h == 1)
        def _():
            back_copy(hb).start()

    @pl.when(h == 1)
    def _():
        each(nz, send, stp_args)

        @pl.loop(0, nz)
        def _(away):
            send(*sta_args(near_first(away)))

    for hb in range(2):

        @pl.loop(0, nz)
        def _(away):
            c = near_first(away)
            arrived(gmid.at[hb, c], gsem.at[hb, c])
            for j in range(2):
                send(*f_args(hb, c, j))
                send(*fe_args(hb, c, j))

    arrived(prow, rsem.at[1])
    arrived(stp, rsem.at[7])
    nchunk = 2 * nz

    @pl.loop(0, nchunk)
    def _(i):
        c = near_first(i // 2)
        hb = i % 2
        m = 2 * c + hb

        @pl.when(hb == 0)
        def _():
            arrived(sta.at[c], stsem.at[c])

        cp = ((m + nchunk - 1) % nchunk) // 2
        cn = ((m + 1) % nchunk) // 2
        tp = (4 * hb + 7) % 8
        tn = (4 * hb + 4) % 8
        y = []
        for b in range(2):
            t = [stp[c, b, 4 * hb + i] for i in range(4)]
            lf, rt = neighbours(
                t, cols_of(stp[cp, b, tp], -1), cols_of(stp[cn, b, tn], 1), lane
            )
            y.append([slopes(t[i], lf[i], rt[i]) for i in range(4)])
        ybefore, ynow = y
        before = [sta[c, 0, e, hb] for e in range(4)]
        now = [sta[c, 1, e, hb] for e in range(4)]
        for k in range(nk):
            mix3 = jnp.broadcast_to(msend[k:k + 1, :], (24, 128))
            wgt3 = jnp.broadcast_to(msend[8 + k:9 + k, :], (24, 128))
            mix, wgt = mix3[0:8], wgt3[0:8]
            keep3 = 1.0 - mix3
            keep = 1.0 - mix
            t = [
                prow[2 * m + i // 2, k, :, pl.ds(128 * (i % 2), 128)] for i in range(4)
            ]
            left = cols_of(prow[(2 * m + ns - 1) % ns, k, :, pl.ds(128, 128)], -1)
            right = cols_of(prow[(2 * m + 2) % ns, k, :, pl.ds(0, 128)], 1)
            lf, rt = neighbours(t, left, right, lane)
            b = [bends(t[i], lf[i], rt[i]) for i in range(4)]
            d1 = mix3 - wgt3 * pack4([x[0] for x in b], sub)
            d2 = mix3 - wgt3 * pack4([x[1] for x in b], sub)
            off = -wgt3 * pack4([x[2] for x in b], sub)
            new = step_forward(now, before, d1, d2, off, keep3)
            before, now = now, new
            for e, x in enumerate(shear_of(new)):
                for i, part in enumerate(unpack4(x, sub)):
                    col = pl.ds(pl.multiple_of(m * 512 + i * 128, 128), 128)
                    sv[k, e, :, col] = part[0:6]
            ynew = []
            for i in range(4):
                sl = slopes(t[i], lf[i], rt[i])
                both = []
                for e in range(2):
                    v = mix * ynow[i][e] + keep * ybefore[i][e] - wgt * sl[e]
                    both.append(v)
                    col = pl.ds(pl.multiple_of(m * 512 + i * 128, 128), 128)
                    dv[k, :, e, col] = v[0:6]
                ynew.append(both)
            ybefore, ynow = ynow, ynew

    arrived(grx, rsem.at[9])
    arrived(gerx, rsem.at[10])

    each(ns, sent, pix_args)
    each(ns, sent, row_args)

    @pl.when(on_edge)
    def _():
        each(ns, sent, edge_args)

    each(nz, sent, meta_args)
    for hb in range(2):
        each(nz, sent, obs_args(hb))

    @pl.loop(0, nz)
    def _(zz):
        @pl.when((h == 1) | (zz > 0))
        def _():
            sent(*sta_args(zz))
            sent(*stp_args(zz))

        for hb in range(2):
            sent(*g_args(hb, zz))
            for j in range(2):
                sent(*f_args(hb, zz, j))
                sent(*fe_args(hb, zz, j))

    @pl.when(h == 0)
    def _():
        chain_copy(ast, 0, rsem.at[4]).wait_send()
        chain_copy(phi, 1, rsem.at[5]).wait_send()

    @pl.when(h == 1)
    def _():
        back_copy(0).wait_send()
        back_copy(1).wait_send()


def finish(nz, ns, nk, dv, sv, grx, gerx, defl, shear, grad, gv, sem):
    sub, lane = iotas()
    odd = lax.axis_index("slab") % 2
    out_s = pltpu.make_async_copy(sv, shear, sem.at[0])
    out_d = pltpu.make_async_copy(dv, defl, sem.at[1])
    out_g = pltpu.make_async_copy(gv, grad, sem.at[2])
    out_s.start()
    out_d.start()

    spot = lane == jnp.where(odd == 1, 127, 0)
    for k in range(nk):
        for t in range(2):
            part = []
            for d in range(ns):
                edge = jnp.broadcast_to(gerx[d][:, k:k + 1], (8, 128))
                part.append(grx[d, 2 * k + t] + jnp.where(spot & (odd == t), edge, 0.0))
            for d in range(ns):
                g = part[d]
                g = g + jnp.where(sub == 1, rows_of(part[(d + ns - 1) % ns], 6), 0.0)
                g = g + jnp.where(sub == 6, rows_of(part[(d + 1) % ns], -6), 0.0)
                gv[k, 6 * d:6 * d + 6, pl.ds(128 * t, 128)] = rows_of(g, 1)[0:6]
    out_g.start()
    out_s.wait()
    out_d.wait()
    out_g.wait()


def on_device(nz, ns, potential, mixing, lens_weight, observed, noise_weight):
    nk, total, width = potential.shape
    rows = total // ns
    wide = ns * width
    per = ns // nz
    last = nz * nk
    anyspec = pl.BlockSpec(memory_space=pl.ANY)
    hbm = pl.BlockSpec(memory_space=pltpu.HBM)
    vmem = pl.BlockSpec(memory_space=pltpu.VMEM)
    smem = pl.BlockSpec(memory_space=pltpu.SMEM)
    v = lambda *shape: pltpu.VMEM(shape, F32)
    dma = lambda *shape: pltpu.SemaphoreType.DMA(shape)
    received = [
        (nk, rows, 2, wide), (nk, 3, rows, wide), (ns, 2 * nk, 8, 128), (ns, 8, 128),
    ]
    stay = lambda x: pltpu.with_memory_space_constraint(x, pltpu.HBM)
    shaped = lambda shape: jax.ShapeDtypeStruct(shape, F32)
    mids = pl.pallas_call(
        functools.partial(exchange, nz, ns, nk),
        out_shape=tuple(shaped(x) for x in received),
        in_specs=[hbm] * 5,
        out_specs=(vmem,) * 4,
        scratch_shapes=[
            pltpu.SMEM((nk,), F32), pltpu.SMEM((nk,), F32),
            v(nk, total, width), v(nk, 3, rows, wide), v(nk, rows, wide),
            v(ns, nk, 8, width), v(ns, 8, 128), v(2, nz, nk, 4, 24, 128),
            v(ns, nk, 8, width), v(nz, 2, 4, 2, 24, 128), v(nz, 2, 8, 8, 128), v(16, 128),
            v(nz, per, nk, 8, width), v(nz, 2, 8, 128), v(nz, 16, 128), v(2, nz, nk, 4, 24, 128),
            v(last + 2, 4, 2, 24, 128), v(last, 3, 2, 24, 128), v(last + 2, 8, 8, 128),
            v(2, 8, 24, 128),
            v(2, nz, 4 * nk + 2, 8, 128), v(2, nz, 4 * nk + 2, 8, 128),
            dma(6), dma(2, ns), dma(ns), dma(nz), dma(2, nz), dma(nz), dma(nz), dma(4),
            dma(2, nz), dma(2, nz, 2), dma(2, nz, 2), dma(11), dma(2, nz), dma(2, nz), dma(2), dma(nz),
        ],
        name="exchange",
        compiler_params=pltpu.CompilerParams(
            collective_id=0, has_side_effects=True, vmem_limit_bytes=24 * 1024 * 1024
        ),
    )(stay(potential), stay(mixing), stay(lens_weight), stay(observed), stay(noise_weight))
    defl, shear, grad = pl.pallas_call(
        functools.partial(finish, nz, ns, nk),
        out_shape=(
            shaped((nk, rows, 2, wide)), shaped((nk, 3, rows, wide)), shaped((nk, total, width)),
        ),
        in_specs=[vmem] * 4,
        out_specs=(hbm,) * 3,
        scratch_shapes=[v(nk, total, width), dma(3)],
        name="finish",
        compiler_params=pltpu.CompilerParams(vmem_limit_bytes=24 * 1024 * 1024),
    )(*mids)
    return jnp.transpose(defl, (0, 2, 1, 3)), shear, grad


def solution(mesh):
    nz = mesh.shape["plane"] // NH
    ns = mesh.shape["slab"]
    placed = (
        P("plane", None, "slab"),
        P("plane"),
        P("plane"),
        P("plane", None, "slab", None),
        P("plane", "slab", None),
    )
    return jax.shard_map(
        functools.partial(on_device, nz, ns),
        mesh=mesh,
        in_specs=placed,
        out_specs=(
            P("plane", None, "slab", None),
            P("plane", None, "slab", None),
            P("plane", None, "slab"),
        ),
        check_vma=False,
    )
```

```python
import functools

import jax
import jax.numpy as jnp
from jax import lax
from jax.experimental import pallas as pl
from jax.experimental.pallas import tpu as pltpu
from jax.sharding import PartitionSpec as P

F32 = jnp.float32
MESH = pl.DeviceIdType.MESH
NH = 2


def rows_of(x, shift):
    return pltpu.roll(x, (-shift) % 8, axis=0)


def cols_of(x, shift):
    return pltpu.roll(x, (-shift) % 128, axis=1)


def iotas():
    return (
        lax.broadcasted_iota(jnp.int32, (8, 128), 0),
        lax.broadcasted_iota(jnp.int32, (8, 128), 1),
    )


def pack4(tiles, sub):
    a, b, c, d = tiles
    return jnp.concatenate(
        [
            jnp.where(sub < 6, a, rows_of(d, -6)),
            jnp.where(sub < 6, b, rows_of(d, -4)),
            jnp.where(sub < 6, c, rows_of(d, -2)),
        ],
        axis=0,
    )


def unpack4(x, sub):
    a, b, c = x[0:8], x[8:16], x[16:24]
    d = jnp.where(
        sub < 2, rows_of(a, -2), jnp.where(sub < 4, rows_of(b, -4), rows_of(c, -6))
    )
    return [a, b, c, d]


def neighbours(tiles, left, right, lane):
    ahead = [cols_of(t, -1) for t in tiles]
    behind = [cols_of(t, 1) for t in tiles]
    n = len(tiles)
    lefts = [jnp.where(lane == 0, left if i == 0 else ahead[i - 1], ahead[i]) for i in range(n)]
    rights = [
        jnp.where(lane == 127, right if i == n - 1 else behind[i + 1], behind[i]) for i in range(n)
    ]
    return lefts, rights


def bends(t, lf, rt):
    mid = rows_of(t, 1)
    down = rows_of(t, 2)
    rr = down - 2.0 * mid + t
    cc = rows_of(rt - 2.0 * t + lf, 1)
    q = 0.25 * (rt - lf)
    return rr, cc, rows_of(q, 2) - q


def slopes(t, lf, rt):
    return 0.5 * (rows_of(t, 2) - t), rows_of(0.5 * (rt - lf), 1)


def step_forward(now, before, d1, d2, off, keep):
    return [
        d1 * now[0] + off * now[2] + keep * before[0],
        d1 * now[1] + off * now[3] + keep * before[1],
        off * now[0] + d2 * now[2] + keep * before[2],
        off * now[1] + d2 * now[3] + keep * before[3],
    ]


def shear_of(a):
    return [1.0 - 0.5 * (a[0] + a[3]), 0.5 * (a[3] - a[0]), -0.5 * (a[1] + a[2])]


def exchange(
    nz, ns, nk,
    pot, mix_hbm, wgt_hbm, obs, noi,
    dv, sv, grx, gerx,
    mix_in, wgt_in, pv, ov, nv, psend, esend, osend,
    prow, sta, stp, msend,
    prx, erx, mrx, orx,
    ast, mst, phi, pq,
    gsend, gmid,
    lsem, ps, es, ms, os_, sas, sps, cs, gs, fs, fes, rsem, osem, gsem, bsem, stsem, entered,
):
    h = lax.axis_index("plane") // nz
    z = lax.axis_index("plane") % nz
    s = lax.axis_index("slab")
    per = ns // nz
    blk = s // per
    pos = s % per
    sub, lane = iotas()

    barrier = pltpu.get_barrier_semaphore()

    @pl.loop(0, ns)
    def _(ss):
        for zz in range(nz):

            @pl.when((zz != z) | (ss != s))
            def _():
                pl.semaphore_signal(
                    barrier, inc=1, device_id={"plane": h * nz + zz, "slab": ss},
                    device_id_type=MESH,
                )

    @pl.when(h == 0)
    def _():
        pl.semaphore_signal(
            barrier, inc=1, device_id={"plane": nz + z, "slab": s}, device_id_type=MESH
        )

    load_p = pltpu.make_async_copy(pot, pv, lsem.at[0])
    load_o = pltpu.make_async_copy(obs, ov, lsem.at[1])
    load_n = pltpu.make_async_copy(noi, nv, lsem.at[2])
    load_m = pltpu.make_async_copy(mix_hbm, mix_in, lsem.at[3])
    load_w = pltpu.make_async_copy(wgt_hbm, wgt_in, lsem.at[4])
    load_p.start()
    load_m.start()
    load_w.start()
    load_o.start()
    load_n.start()

    def remote(src, dst, ssem, r, zz, ss):
        return pltpu.make_async_remote_copy(
            src_ref=src, dst_ref=dst, send_sem=ssem, recv_sem=r,
            device_id={"plane": h * nz + zz, "slab": ss}, device_id_type=MESH,
        )

    def send(src, dst, ssem, r, zz, ss):
        own = (zz == z) & (ss == s)

        @pl.when(jnp.logical_not(own))
        def _():
            remote(src, dst, ssem, r, zz, ss).start()

        @pl.when(own)
        def _():
            pltpu.make_async_copy(src, dst, r).start()

    def sent(src, dst, ssem, r, zz, ss):
        @pl.when((zz != z) | (ss != s))
        def _():
            remote(src, dst, ssem, r, zz, ss).wait_send()

    def arrived(buf, r):
        pltpu.make_async_copy(buf, buf, r).wait()

    load_p.wait()
    total = 6 * ns
    for d in range(ns):
        edge = jnp.zeros((8, 128), F32)
        for k in range(nk):
            for t in range(2):
                cols = pl.ds(128 * t, 128)
                if d == 0:
                    v = jnp.where(
                        sub == 0, pv[k, total - 8:total, cols][7:8], rows_of(pv[k, 0:8, cols], -1)
                    )
                elif d == ns - 1:
                    v = jnp.where(
                        sub == 7, pv[k, 0:8, cols][0:1], rows_of(pv[k, total - 8:total, cols], 1)
                    )
                else:
                    v = pv[k, 6 * d - 1:6 * d + 7, cols]
                psend[d, k, :, cols] = v
                if t == 0:
                    first = jnp.broadcast_to(v[:, 0:1], (8, 128))
                else:
                    last = jnp.broadcast_to(v[:, 127:128], (8, 128))
            edge = jnp.where(lane == k, jnp.where(pos == 0, first, last), edge)
        esend[d] = edge
    load_m.wait()
    load_w.wait()
    for k in range(nk):
        msend[k:k + 1, :] = jnp.full((1, 128), mix_in[k], F32)
        msend[8 + k:9 + k, :] = jnp.full((1, 128), wgt_in[k], F32)

    @pl.when(h == 0)
    def _():
        pl.semaphore_wait(barrier, nz * ns - 1)

    @pl.when(h == 1)
    def _():
        pl.semaphore_wait(barrier, nz * ns)
        pl.semaphore_signal(
            entered, inc=1, device_id={"plane": z, "slab": s}, device_id_type=MESH
        )

    eblk = jnp.where(pos == 0, (blk + nz - 1) % nz, (blk + 1) % nz)
    eside = jnp.where(pos == 0, 1, 0)
    on_edge = (pos == 0) | (pos == per - 1)

    def each(n, fn, args):
        first = s if n == ns else z

        @pl.loop(0, n)
        def _(i):
            fn(*args((first + i) % n))

    pix_args = lambda d: (psend.at[d], prx.at[z, pos], ps.at[0, d], rsem.at[0], blk, d)
    row_args = lambda d: (psend.at[d], prow.at[s], ps.at[1, d], rsem.at[1], z, d)
    edge_args = lambda d: (esend.at[d], erx.at[z, eside], es.at[d], rsem.at[2], eblk, d)
    meta_args = lambda d: (msend, mrx.at[z], ms.at[d], rsem.at[3], d, s)
    obs_args = lambda hb: lambda d: (
        osend.at[hb, d], orx.at[hb, z], os_.at[hb, d], osem.at[hb, z], d, s
    )

    each(ns, send, pix_args)

    @pl.when(on_edge)
    def _():
        each(ns, send, edge_args)

    each(nz, send, meta_args)

    load_o.wait()
    load_n.wait()

    for hb in range(2):

        @pl.loop(0, nz)
        def _(d):
            for k in range(nk):
                for a in range(4):
                    t = []
                    for i in range(4):
                        c = pl.ds(pl.multiple_of(d * 1024 + (hb * 4 + i) * 128, 128), 128)
                        t.append(ov[k, a, :, c] if a < 3 else nv[k, :, c])
                    for i in range(3):
                        osend[hb, d, k, a, pl.ds(8 * i, 8), :] = jnp.concatenate(
                            [t[i], t[3][2 * i:2 * i + 2]], axis=0
                        )

        each(nz, send, obs_args(hb))

    each(ns, send, row_args)

    @pl.when(h == 0)
    def _():
        one = jnp.ones((2, 24, 128), F32)
        zero = jnp.zeros((2, 24, 128), F32)
        for i in range(2):
            ast[i, 0] = one
            ast[i, 1] = zero
            ast[i, 2] = zero
            ast[i, 3] = one
            phi[i] = jnp.zeros((8, 8, 128), F32)

    arrived(prx, rsem.at[0])
    arrived(erx, rsem.at[2])
    arrived(mrx, rsem.at[3])

    last = nz * nk

    def chain_copy(buf, i, r):
        return pltpu.make_async_remote_copy(
            src_ref=buf.at[pl.ds(last, 2)], dst_ref=buf.at[pl.ds(0, 2)],
            send_sem=cs.at[i], recv_sem=r,
            device_id={"plane": nz + z, "slab": s}, device_id_type=MESH,
        )

    @pl.when(h == 1)
    def _():
        arrived(ast.at[pl.ds(0, 2)], rsem.at[4])

    sta_args = lambda q: (ast.at[pl.ds(nk * q, 2)], sta.at[z], sas.at[q], stsem.at[z], q, s)
    stp_args = lambda q: (phi.at[pl.ds(nk * q, 2)], stp.at[z], sps.at[q], rsem.at[7], q, s)

    @pl.loop(0, nz)
    def _(zz):
        for k in range(nk):
            kk = zz * nk + k
            mix = jnp.broadcast_to(mrx[zz, k:k + 1, :], (8, 128))
            wgt = jnp.broadcast_to(mrx[zz, 8 + k:9 + k, :], (8, 128))
            mix3 = jnp.concatenate([mix] * 3, axis=0)
            wgt3 = jnp.concatenate([wgt] * 3, axis=0)
            keep3 = 1.0 - mix3
            left = jnp.broadcast_to(erx[zz, 0][:, k:k + 1], (8, 128))
            right = jnp.broadcast_to(erx[zz, 1][:, k:k + 1], (8, 128))
            tiles = [prx[zz, i // 2, k, :, pl.ds(128 * (i % 2), 128)] for i in range(8)]
            lefts, rights = neighbours(tiles, left, right, lane)
            for hb in range(2):
                b = [bends(tiles[i], lefts[i], rights[i]) for i in range(4 * hb, 4 * hb + 4)]
                d1 = mix3 - wgt3 * pack4([x[0] for x in b], sub)
                d2 = mix3 - wgt3 * pack4([x[1] for x in b], sub)
                off = -wgt3 * pack4([x[2] for x in b], sub)
                mst[kk, 0, hb] = d1
                mst[kk, 1, hb] = d2
                mst[kk, 2, hb] = off
                now = [ast[kk + 1, c, hb] for c in range(4)]
                before = [ast[kk, c, hb] for c in range(4)]
                new = step_forward(now, before, d1, d2, off, keep3)
                for c in range(4):
                    ast[kk + 2, c, hb] = new[c]
        @pl.when((h == 0) & (zz > 0) & ((zz + nz - z) % nz != 2))
        def _():
            send(*sta_args(zz))

    def potential_sum():
        @pl.loop(0, nz)
        def _(zz):
            for k in range(nk):
                kk = zz * nk + k
                mix = jnp.broadcast_to(mrx[zz, k:k + 1, :], (8, 128))
                wgt = jnp.broadcast_to(mrx[zz, 8 + k:9 + k, :], (8, 128))
                keep = 1.0 - mix
                for i in range(8):
                    p = prx[zz, i // 2, k, :, pl.ds(128 * (i % 2), 128)]
                    phi[kk + 2, i] = mix * phi[kk + 1, i] + keep * phi[kk, i] - wgt * p

    @pl.when(h == 0)
    def _():
        pl.semaphore_wait(entered, 1)
        chain_copy(ast, 0, rsem.at[4]).start()

    @pl.when(h == 1)
    def _():
        arrived(phi.at[pl.ds(0, 2)], rsem.at[5])

    potential_sum()

    @pl.when(h == 0)
    def _():
        chain_copy(phi, 1, rsem.at[5]).start()

        @pl.loop(1, nz)
        def _(q):
            send(*stp_args(q))

    @pl.when((h == 0) & (z == 0))
    def _():
        for c in range(nz):
            pltpu.make_async_copy(ast.at[pl.ds(0, 2)], sta.at[c], stsem.at[c]).start()
            pltpu.make_async_copy(phi.at[pl.ds(0, 2)], stp.at[c], rsem.at[7]).start()

    def near_first(i):
        return (z + jnp.where(i == 2, 3, jnp.where(i == 3, 2, i))) % nz

    def back_copy(hb):
        return pltpu.make_async_remote_copy(
            src_ref=pq.at[hb], dst_ref=pq.at[hb], send_sem=cs.at[2 + hb], recv_sem=bsem.at[hb],
            device_id={"plane": z, "slab": s}, device_id_type=MESH,
        )

    @pl.when(h == 1)
    def _():
        pq[...] = jnp.zeros(pq.shape, F32)

    g_args = lambda hb, zz: (
        gsend.at[hb, zz], gmid.at[hb, z], gs.at[hb, zz], gsem.at[hb, z], zz, s
    )
    tiles_of = 2 * nk

    f_args = lambda hb, c, j: (
        gmid.at[hb, c, pl.ds(j * tiles_of, tiles_of)], grx.at[s], fs.at[hb, c, j], rsem.at[9],
        z, c * per + hb * 2 + j,
    )
    fe_args = lambda hb, c, e: (
        gmid.at[hb, c, 2 * tiles_of], gerx.at[s], fes.at[hb, c, e], rsem.at[10],
        z, (c * per + hb * 2 + (2 if e else ns - 1)) % ns,
    )

    zero8 = jnp.zeros((8, 128), F32)
    inner = (sub >= 1) & (sub <= 6)

    for hb in range(2):
        for d in range(nz):
            arrived(orx.at[hb, d], osem.at[hb, d])

        @pl.when(h == 0)
        def _():
            arrived(pq.at[hb], bsem.at[hb])

        @pl.loop(0, nz)
        def _(back):
            zz = nz - 1 - back
            edges = zero8
            for k in reversed(range(nk)):
                kk = zz * nk + k
                mix = jnp.broadcast_to(mrx[zz, k:k + 1, :], (24, 128))
                nwt = -jnp.broadcast_to(mrx[zz, 8 + k:9 + k, :], (24, 128))
                keep = 1.0 - mix
                nxt = [ast[kk + 2, c, hb] for c in range(4)]
                a = [ast[kk + 1, c, hb] for c in range(4)]
                nw = orx[hb, zz, k, 3]
                r = [nw * (m - orx[hb, zz, k, c]) for c, m in enumerate(shear_of(nxt))]
                tilt = -0.5 * r[2]
                f = [
                    pq[hb, 0] - 0.5 * (r[0] + r[1]),
                    pq[hb, 1] + tilt,
                    pq[hb, 2] + tilt,
                    pq[hb, 3] - 0.5 * (r[0] - r[1]),
                ]
                d1, d2, off = mst[kk, 0, hb], mst[kk, 1, hb], mst[kk, 2, hb]
                pq[hb, 0] = d1 * f[0] + off * f[2] + pq[hb, 4]
                pq[hb, 1] = d1 * f[1] + off * f[3] + pq[hb, 5]
                pq[hb, 2] = off * f[0] + d2 * f[2] + pq[hb, 6]
                pq[hb, 3] = off * f[1] + d2 * f[3] + pq[hb, 7]
                for c in range(4):
                    pq[hb, 4 + c] = keep * f[c]
                c0 = unpack4(nwt * (f[0] * a[0] + f[1] * a[1]), sub)
                c1 = unpack4(nwt * (f[2] * a[2] + f[3] * a[3]), sub)
                c2 = unpack4(nwt * (f[0] * a[2] + f[1] * a[3] + f[2] * a[0] + f[3] * a[1]), sub)
                c0 = [jnp.where(inner, rows_of(t, -1), 0.0) for t in c0]
                c1 = [jnp.where(inner, rows_of(t, -1), 0.0) for t in c1]
                c2 = [jnp.where(inner, rows_of(t, -1), 0.0) for t in c2]
                l1, r1 = neighbours(c1, zero8, zero8, lane)
                l2, r2 = neighbours(c2, zero8, zero8, lane)
                for i in range(4):
                    q = 0.25 * (r2[i] - l2[i])
                    gsend[hb, zz, (i // 2) * tiles_of + 2 * k + i % 2] = (
                        rows_of(c0[i], 1) - 2.0 * c0[i] + rows_of(c0[i], -1)
                        + (r1[i] - 2.0 * c1[i] + l1[i])
                        + (rows_of(q, 1) - rows_of(q, -1))
                    )
                vl = c1[0] + 0.25 * (rows_of(c2[0], 1) - rows_of(c2[0], -1))
                vr = c1[3] - 0.25 * (rows_of(c2[3], 1) - rows_of(c2[3], -1))
                edges = jnp.where(lane == k, jnp.broadcast_to(vl[:, 0:1], (8, 128)), edges)
                edges = jnp.where(lane == 8 + k, jnp.broadcast_to(vr[:, 127:128], (8, 128)), edges)
            gsend[hb, zz, 2 * tiles_of] = edges
            send(*g_args(hb, zz))

        @pl.when(h == 1)
        def _():
            back_copy(hb).start()

    @pl.when(h == 1)
    def _():
        each(nz, send, stp_args)

        @pl.loop(0, nz)
        def _(away):
            send(*sta_args(near_first(away)))

    @pl.when((h == 0) & (z != 2))
    def _():
        send(*sta_args((z + 2) % nz))

    for hb in range(2):

        @pl.loop(0, nz)
        def _(away):
            c = near_first(away)
            arrived(gmid.at[hb, c], gsem.at[hb, c])
            for j in range(2):
                send(*f_args(hb, c, j))
                send(*fe_args(hb, c, j))

    each(ns, sent, pix_args)
    each(ns, sent, row_args)

    @pl.when(on_edge)
    def _():
        each(ns, sent, edge_args)

    each(nz, sent, meta_args)
    for hb in range(2):
        each(nz, sent, obs_args(hb))

    arrived(prow, rsem.at[1])
    arrived(stp, rsem.at[7])
    nchunk = 2 * nz

    @pl.loop(0, nchunk)
    def _(i):
        c = near_first(i // 2)
        hb = i % 2
        m = 2 * c + hb

        @pl.when(hb == 0)
        def _():
            arrived(sta.at[c], stsem.at[c])

        cp = ((m + nchunk - 1) % nchunk) // 2
        cn = ((m + 1) % nchunk) // 2
        tp = (4 * hb + 7) % 8
        tn = (4 * hb + 4) % 8
        y = []
        for b in range(2):
            t = [stp[c, b, 4 * hb + i] for i in range(4)]
            lf, rt = neighbours(
                t, cols_of(stp[cp, b, tp], -1), cols_of(stp[cn, b, tn], 1), lane
            )
            y.append([slopes(t[i], lf[i], rt[i]) for i in range(4)])
        ybefore, ynow = y
        before = [sta[c, 0, e, hb] for e in range(4)]
        now = [sta[c, 1, e, hb] for e in range(4)]
        for k in range(nk):
            mix3 = jnp.broadcast_to(msend[k:k + 1, :], (24, 128))
            wgt3 = jnp.broadcast_to(msend[8 + k:9 + k, :], (24, 128))
            mix, wgt = mix3[0:8], wgt3[0:8]
            keep3 = 1.0 - mix3
            keep = 1.0 - mix
            t = [
                prow[2 * m + i // 2, k, :, pl.ds(128 * (i % 2), 128)] for i in range(4)
            ]
            left = cols_of(prow[(2 * m + ns - 1) % ns, k, :, pl.ds(128, 128)], -1)
            right = cols_of(prow[(2 * m + 2) % ns, k, :, pl.ds(0, 128)], 1)
            lf, rt = neighbours(t, left, right, lane)
            b = [bends(t[i], lf[i], rt[i]) for i in range(4)]
            d1 = mix3 - wgt3 * pack4([x[0] for x in b], sub)
            d2 = mix3 - wgt3 * pack4([x[1] for x in b], sub)
            off = -wgt3 * pack4([x[2] for x in b], sub)
            new = step_forward(now, before, d1, d2, off, keep3)
            before, now = now, new
            for e, x in enumerate(shear_of(new)):
                for i, part in enumerate(unpack4(x, sub)):
                    col = pl.ds(pl.multiple_of(m * 512 + i * 128, 128), 128)
                    sv[k, e, :, col] = part[0:6]
            ynew = []
            for i in range(4):
                sl = slopes(t[i], lf[i], rt[i])
                both = []
                for e in range(2):
                    v = mix * ynow[i][e] + keep * ybefore[i][e] - wgt * sl[e]
                    both.append(v)
                    col = pl.ds(pl.multiple_of(m * 512 + i * 128, 128), 128)
                    dv[k, :, e, col] = v[0:6]
                ynew.append(both)
            ybefore, ynow = ynow, ynew

    arrived(grx, rsem.at[9])
    arrived(gerx, rsem.at[10])

    @pl.loop(0, nz)
    def _(zz):
        @pl.when((h == 1) | (zz > 0))
        def _():
            sent(*sta_args(zz))
            sent(*stp_args(zz))

        for hb in range(2):
            sent(*g_args(hb, zz))
            for j in range(2):
                sent(*f_args(hb, zz, j))
                sent(*fe_args(hb, zz, j))

    @pl.when(h == 0)
    def _():
        chain_copy(ast, 0, rsem.at[4]).wait_send()
        chain_copy(phi, 1, rsem.at[5]).wait_send()

    @pl.when(h == 1)
    def _():
        back_copy(0).wait_send()
        back_copy(1).wait_send()


def finish(nz, ns, nk, dv, sv, grx, gerx, defl, shear, grad, gv, sem):
    sub, lane = iotas()
    odd = lax.axis_index("slab") % 2
    out_s = pltpu.make_async_copy(sv, shear, sem.at[0])
    out_d = pltpu.make_async_copy(dv, defl, sem.at[1])
    out_g = pltpu.make_async_copy(gv, grad, sem.at[2])
    out_s.start()
    out_d.start()

    spot = lane == jnp.where(odd == 1, 127, 0)
    for k in range(nk):
        for t in range(2):
            part = []
            for d in range(ns):
                edge = jnp.broadcast_to(
                    jnp.where(odd == 1, gerx[d][:, k:k + 1], gerx[d][:, 8 + k:9 + k]), (8, 128)
                )
                part.append(grx[d, 2 * k + t] + jnp.where(spot & (odd == t), edge, 0.0))
            for d in range(ns):
                g = part[d]
                g = g + jnp.where(sub == 1, rows_of(part[(d + ns - 1) % ns], 6), 0.0)
                g = g + jnp.where(sub == 6, rows_of(part[(d + 1) % ns], -6), 0.0)
                gv[k, 6 * d:6 * d + 6, pl.ds(128 * t, 128)] = rows_of(g, 1)[0:6]
    out_g.start()
    out_s.wait()
    out_d.wait()
    out_g.wait()


def on_device(nz, ns, potential, mixing, lens_weight, observed, noise_weight):
    nk, total, width = potential.shape
    rows = total // ns
    wide = ns * width
    per = ns // nz
    last = nz * nk
    anyspec = pl.BlockSpec(memory_space=pl.ANY)
    hbm = pl.BlockSpec(memory_space=pltpu.HBM)
    vmem = pl.BlockSpec(memory_space=pltpu.VMEM)
    smem = pl.BlockSpec(memory_space=pltpu.SMEM)
    v = lambda *shape: pltpu.VMEM(shape, F32)
    dma = lambda *shape: pltpu.SemaphoreType.DMA(shape)
    received = [
        (nk, rows, 2, wide), (nk, 3, rows, wide), (ns, 2 * nk, 8, 128), (ns, 8, 128),
    ]
    stay = lambda x: pltpu.with_memory_space_constraint(x, pltpu.HBM)
    shaped = lambda shape: jax.ShapeDtypeStruct(shape, F32)
    mids = pl.pallas_call(
        functools.partial(exchange, nz, ns, nk),
        out_shape=tuple(shaped(x) for x in received),
        in_specs=[hbm] * 5,
        out_specs=(vmem,) * 4,
        scratch_shapes=[
            pltpu.SMEM((nk,), F32), pltpu.SMEM((nk,), F32),
            v(nk, total, width), v(nk, 3, rows, wide), v(nk, rows, wide),
            v(ns, nk, 8, width), v(ns, 8, 128), v(2, nz, nk, 4, 24, 128),
            v(ns, nk, 8, width), v(nz, 2, 4, 2, 24, 128), v(nz, 2, 8, 8, 128), v(16, 128),
            v(nz, per, nk, 8, width), v(nz, 2, 8, 128), v(nz, 16, 128), v(2, nz, nk, 4, 24, 128),
            v(last + 2, 4, 2, 24, 128), v(last, 3, 2, 24, 128), v(last + 2, 8, 8, 128),
            v(2, 8, 24, 128),
            v(2, nz, 4 * nk + 1, 8, 128), v(2, nz, 4 * nk + 1, 8, 128),
            dma(6), dma(2, ns), dma(ns), dma(nz), dma(2, nz), dma(nz), dma(nz), dma(4),
            dma(2, nz), dma(2, nz, 2), dma(2, nz, 2), dma(11), dma(2, nz), dma(2, nz), dma(2), dma(nz),
            pltpu.SemaphoreType.REGULAR,
        ],
        name="exchange",
        compiler_params=pltpu.CompilerParams(
            collective_id=0, has_side_effects=True, vmem_limit_bytes=24 * 1024 * 1024
        ),
    )(stay(potential), stay(mixing), stay(lens_weight), stay(observed), stay(noise_weight))
    defl, shear, grad = pl.pallas_call(
        functools.partial(finish, nz, ns, nk),
        out_shape=(
            shaped((nk, rows, 2, wide)), shaped((nk, 3, rows, wide)), shaped((nk, total, width)),
        ),
        in_specs=[vmem] * 4,
        out_specs=(hbm,) * 3,
        scratch_shapes=[v(nk, total, width), dma(3)],
        name="finish",
        compiler_params=pltpu.CompilerParams(vmem_limit_bytes=24 * 1024 * 1024),
    )(*mids)
    return jnp.transpose(defl, (0, 2, 1, 3)), shear, grad


def solution(mesh):
    nz = mesh.shape["plane"] // NH
    ns = mesh.shape["slab"]
    placed = (
        P("plane", None, "slab"),
        P("plane"),
        P("plane"),
        P("plane", None, "slab", None),
        P("plane", "slab", None),
    )
    return jax.shard_map(
        functools.partial(on_device, nz, ns),
        mesh=mesh,
        in_specs=placed,
        out_specs=(
            P("plane", None, "slab", None),
            P("plane", None, "slab", None),
            P("plane", None, "slab"),
        ),
        check_vma=False,
    )
```

```python
import functools

import jax
import jax.numpy as jnp
from jax import lax
from jax.experimental import pallas as pl
from jax.experimental.pallas import tpu as pltpu
from jax.sharding import PartitionSpec as P

F32 = jnp.float32
MESH = pl.DeviceIdType.MESH
NH = 2


def rows_of(x, shift):
    return pltpu.roll(x, (-shift) % 8, axis=0)


def cols_of(x, shift):
    return pltpu.roll(x, (-shift) % 128, axis=1)


def iotas():
    return (
        lax.broadcasted_iota(jnp.int32, (8, 128), 0),
        lax.broadcasted_iota(jnp.int32, (8, 128), 1),
    )


def pack4(tiles, sub):
    a, b, c, d = tiles
    return jnp.concatenate(
        [
            jnp.where(sub < 6, a, rows_of(d, -6)),
            jnp.where(sub < 6, b, rows_of(d, -4)),
            jnp.where(sub < 6, c, rows_of(d, -2)),
        ],
        axis=0,
    )


def unpack4(x, sub):
    a, b, c = x[0:8], x[8:16], x[16:24]
    d = jnp.where(
        sub < 2, rows_of(a, -2), jnp.where(sub < 4, rows_of(b, -4), rows_of(c, -6))
    )
    return [a, b, c, d]


def neighbours(tiles, left, right, lane):
    ahead = [cols_of(t, -1) for t in tiles]
    behind = [cols_of(t, 1) for t in tiles]
    n = len(tiles)
    lefts = [jnp.where(lane == 0, left if i == 0 else ahead[i - 1], ahead[i]) for i in range(n)]
    rights = [
        jnp.where(lane == 127, right if i == n - 1 else behind[i + 1], behind[i]) for i in range(n)
    ]
    return lefts, rights


def bends(t, lf, rt):
    mid = rows_of(t, 1)
    down = rows_of(t, 2)
    rr = down - 2.0 * mid + t
    cc = rows_of(rt - 2.0 * t + lf, 1)
    q = 0.25 * (rt - lf)
    return rr, cc, rows_of(q, 2) - q


def slopes(t, lf, rt):
    return 0.5 * (rows_of(t, 2) - t), rows_of(0.5 * (rt - lf), 1)


def step_forward(now, before, d1, d2, off, keep):
    return [
        d1 * now[0] + off * now[2] + keep * before[0],
        d1 * now[1] + off * now[3] + keep * before[1],
        off * now[0] + d2 * now[2] + keep * before[2],
        off * now[1] + d2 * now[3] + keep * before[3],
    ]


def shear_of(a):
    return [1.0 - 0.5 * (a[0] + a[3]), 0.5 * (a[3] - a[0]), -0.5 * (a[1] + a[2])]


def exchange(
    nz, ns, nk,
    pot, mix_hbm, wgt_hbm, obs, noi,
    dv, sv, grx, gerx,
    mix_in, wgt_in, pv, ov, nv, psend, esend, osend,
    prow, sta, stp, msend,
    prx, erx, mrx, orx,
    ast, mst, phi, pq,
    gsend, gmid,
    lsem, ps, es, ms, os_, sas, sps, cs, gs, fs, fes, rsem, osem, gsem, bsem, stsem, entered,
):
    h = lax.axis_index("plane") // nz
    z = lax.axis_index("plane") % nz
    s = lax.axis_index("slab")
    per = ns // nz
    blk = s // per
    pos = s % per
    sub, lane = iotas()

    load_p = pltpu.make_async_copy(pot, pv, lsem.at[0])
    load_o = pltpu.make_async_copy(obs, ov, lsem.at[1])
    load_n = pltpu.make_async_copy(noi, nv, lsem.at[2])
    load_m = pltpu.make_async_copy(mix_hbm, mix_in, lsem.at[3])
    load_w = pltpu.make_async_copy(wgt_hbm, wgt_in, lsem.at[4])
    load_p.start()
    load_m.start()
    load_w.start()
    load_o.start()
    load_n.start()

    barrier = pltpu.get_barrier_semaphore()

    @pl.loop(0, ns)
    def _(ss):
        for zz in range(nz):

            @pl.when((zz != z) | (ss != s))
            def _():
                pl.semaphore_signal(
                    barrier, inc=1, device_id={"plane": h * nz + zz, "slab": ss},
                    device_id_type=MESH,
                )

    @pl.when(h == 0)
    def _():
        pl.semaphore_signal(
            barrier, inc=1, device_id={"plane": nz + z, "slab": s}, device_id_type=MESH
        )

    def remote(src, dst, ssem, r, zz, ss):
        return pltpu.make_async_remote_copy(
            src_ref=src, dst_ref=dst, send_sem=ssem, recv_sem=r,
            device_id={"plane": h * nz + zz, "slab": ss}, device_id_type=MESH,
        )

    def send(src, dst, ssem, r, zz, ss):
        own = (zz == z) & (ss == s)

        @pl.when(jnp.logical_not(own))
        def _():
            remote(src, dst, ssem, r, zz, ss).start()

        @pl.when(own)
        def _():
            pltpu.make_async_copy(src, dst, r).start()

    def sent(src, dst, ssem, r, zz, ss):
        @pl.when((zz != z) | (ss != s))
        def _():
            remote(src, dst, ssem, r, zz, ss).wait_send()

    def arrived(buf, r):
        pltpu.make_async_copy(buf, buf, r).wait()

    load_p.wait()
    total = 6 * ns
    for d in range(ns):
        edge = jnp.zeros((8, 128), F32)
        for k in range(nk):
            for t in range(2):
                cols = pl.ds(128 * t, 128)
                if d == 0:
                    v = jnp.where(
                        sub == 0, pv[k, total - 8:total, cols][7:8], rows_of(pv[k, 0:8, cols], -1)
                    )
                elif d == ns - 1:
                    v = jnp.where(
                        sub == 7, pv[k, 0:8, cols][0:1], rows_of(pv[k, total - 8:total, cols], 1)
                    )
                else:
                    v = pv[k, 6 * d - 1:6 * d + 7, cols]
                psend[d, k, :, cols] = v
                if t == 0:
                    first = jnp.broadcast_to(v[:, 0:1], (8, 128))
                else:
                    last = jnp.broadcast_to(v[:, 127:128], (8, 128))
            edge = jnp.where(lane == k, jnp.where(pos == 0, first, last), edge)
        esend[d] = edge
    load_m.wait()
    load_w.wait()
    for k in range(nk):
        msend[k:k + 1, :] = jnp.full((1, 128), mix_in[k], F32)
        msend[8 + k:9 + k, :] = jnp.full((1, 128), wgt_in[k], F32)

    @pl.when(h == 0)
    def _():
        pl.semaphore_wait(barrier, nz * ns - 1)

    @pl.when(h == 1)
    def _():
        pl.semaphore_wait(barrier, nz * ns)
        pl.semaphore_signal(
            entered, inc=1, device_id={"plane": z, "slab": s}, device_id_type=MESH
        )

    eblk = jnp.where(pos == 0, (blk + nz - 1) % nz, (blk + 1) % nz)
    eside = jnp.where(pos == 0, 1, 0)
    on_edge = (pos == 0) | (pos == per - 1)

    def each(n, fn, args):
        first = s if n == ns else z

        @pl.loop(0, n)
        def _(i):
            away = (i + 1) // 2 * (2 * (i % 2) - 1)
            fn(*args((first + n + away) % n))

    pix_args = lambda d: (psend.at[d], prx.at[z, pos], ps.at[0, d], rsem.at[0], blk, d)
    row_args = lambda d: (psend.at[d], prow.at[s], ps.at[1, d], rsem.at[1], z, d)
    edge_args = lambda d: (esend.at[d], erx.at[z, eside], es.at[d], rsem.at[2], eblk, d)
    meta_args = lambda d: (msend, mrx.at[z], ms.at[d], rsem.at[3], d, s)
    obs_args = lambda hb: lambda d: (
        osend.at[hb, d], orx.at[hb, z], os_.at[hb, d], osem.at[hb, z], d, s
    )

    each(ns, send, pix_args)

    @pl.when(on_edge)
    def _():
        each(ns, send, edge_args)

    each(nz, send, meta_args)

    load_o.wait()
    load_n.wait()

    for hb in range(2):

        @pl.loop(0, nz)
        def _(d):
            for k in range(nk):
                for a in range(4):
                    t = []
                    for i in range(4):
                        c = pl.ds(pl.multiple_of(d * 1024 + (hb * 4 + i) * 128, 128), 128)
                        t.append(ov[k, a, :, c] if a < 3 else nv[k, :, c])
                    for i in range(3):
                        osend[hb, d, k, a, pl.ds(8 * i, 8), :] = jnp.concatenate(
                            [t[i], t[3][2 * i:2 * i + 2]], axis=0
                        )

        each(nz, send, obs_args(hb))

    each(ns, send, row_args)

    @pl.when(h == 0)
    def _():
        one = jnp.ones((2, 24, 128), F32)
        zero = jnp.zeros((2, 24, 128), F32)
        for i in range(2):
            ast[i, 0] = one
            ast[i, 1] = zero
            ast[i, 2] = zero
            ast[i, 3] = one
            phi[i] = jnp.zeros((8, 8, 128), F32)

    arrived(prx, rsem.at[0])
    arrived(erx, rsem.at[2])
    arrived(mrx, rsem.at[3])

    last = nz * nk

    def chain_copy(buf, i, r):
        return pltpu.make_async_remote_copy(
            src_ref=buf.at[pl.ds(last, 2)], dst_ref=buf.at[pl.ds(0, 2)],
            send_sem=cs.at[i], recv_sem=r,
            device_id={"plane": nz + z, "slab": s}, device_id_type=MESH,
        )

    @pl.when(h == 1)
    def _():
        arrived(ast.at[pl.ds(0, 2)], rsem.at[4])

    sta_args = lambda q: (ast.at[pl.ds(nk * q, 2)], sta.at[z], sas.at[q], stsem.at[z], q, s)
    stp_args = lambda q: (phi.at[pl.ds(nk * q, 2)], stp.at[z], sps.at[q], rsem.at[7], q, s)

    @pl.loop(0, nz)
    def _(zz):
        for k in range(nk):
            kk = zz * nk + k
            mix = jnp.broadcast_to(mrx[zz, k:k + 1, :], (8, 128))
            wgt = jnp.broadcast_to(mrx[zz, 8 + k:9 + k, :], (8, 128))
            mix3 = jnp.concatenate([mix] * 3, axis=0)
            wgt3 = jnp.concatenate([wgt] * 3, axis=0)
            keep3 = 1.0 - mix3
            left = jnp.broadcast_to(erx[zz, 0][:, k:k + 1], (8, 128))
            right = jnp.broadcast_to(erx[zz, 1][:, k:k + 1], (8, 128))
            tiles = [prx[zz, i // 2, k, :, pl.ds(128 * (i % 2), 128)] for i in range(8)]
            lefts, rights = neighbours(tiles, left, right, lane)
            for hb in range(2):
                b = [bends(tiles[i], lefts[i], rights[i]) for i in range(4 * hb, 4 * hb + 4)]
                d1 = mix3 - wgt3 * pack4([x[0] for x in b], sub)
                d2 = mix3 - wgt3 * pack4([x[1] for x in b], sub)
                off = -wgt3 * pack4([x[2] for x in b], sub)
                mst[kk, 0, hb] = d1
                mst[kk, 1, hb] = d2
                mst[kk, 2, hb] = off
                now = [ast[kk + 1, c, hb] for c in range(4)]
                before = [ast[kk, c, hb] for c in range(4)]
                new = step_forward(now, before, d1, d2, off, keep3)
                for c in range(4):
                    ast[kk + 2, c, hb] = new[c]
        @pl.when((h == 0) & (zz > 0) & ((zz + nz - z) % nz != 2))
        def _():
            send(*sta_args(zz))

    def potential_sum():
        @pl.loop(0, nz)
        def _(zz):
            for k in range(nk):
                kk = zz * nk + k
                mix = jnp.broadcast_to(mrx[zz, k:k + 1, :], (8, 128))
                wgt = jnp.broadcast_to(mrx[zz, 8 + k:9 + k, :], (8, 128))
                keep = 1.0 - mix
                for i in range(8):
                    p = prx[zz, i // 2, k, :, pl.ds(128 * (i % 2), 128)]
                    phi[kk + 2, i] = mix * phi[kk + 1, i] + keep * phi[kk, i] - wgt * p

    @pl.when(h == 0)
    def _():
        pl.semaphore_wait(entered, 1)
        chain_copy(ast, 0, rsem.at[4]).start()

    @pl.when(h == 1)
    def _():
        arrived(phi.at[pl.ds(0, 2)], rsem.at[5])

    potential_sum()

    @pl.when(h == 0)
    def _():
        chain_copy(phi, 1, rsem.at[5]).start()

        @pl.loop(1, nz)
        def _(q):
            send(*stp_args(q))

    @pl.when((h == 0) & (z == 0))
    def _():
        for c in range(nz):
            pltpu.make_async_copy(ast.at[pl.ds(0, 2)], sta.at[c], stsem.at[c]).start()
            pltpu.make_async_copy(phi.at[pl.ds(0, 2)], stp.at[c], rsem.at[7]).start()

    def near_first(i):
        return (z + jnp.where(i == 2, 3, jnp.where(i == 3, 2, i))) % nz

    def back_copy(hb):
        return pltpu.make_async_remote_copy(
            src_ref=pq.at[hb], dst_ref=pq.at[hb], send_sem=cs.at[2 + hb], recv_sem=bsem.at[hb],
            device_id={"plane": z, "slab": s}, device_id_type=MESH,
        )

    @pl.when(h == 1)
    def _():
        pq[...] = jnp.zeros(pq.shape, F32)

    g_args = lambda hb, zz: (
        gsend.at[hb, zz], gmid.at[hb, z], gs.at[hb, zz], gsem.at[hb, z], zz, s
    )
    tiles_of = 2 * nk

    f_args = lambda hb, c, j: (
        gmid.at[hb, c, pl.ds(j * tiles_of, tiles_of)], grx.at[s], fs.at[hb, c, j], rsem.at[9],
        z, c * per + hb * 2 + j,
    )
    fe_args = lambda hb, c, e: (
        gmid.at[hb, c, 2 * tiles_of], gerx.at[s], fes.at[hb, c, e], rsem.at[10],
        z, (c * per + hb * 2 + (2 if e else ns - 1)) % ns,
    )

    zero8 = jnp.zeros((8, 128), F32)
    inner = (sub >= 1) & (sub <= 6)

    for hb in range(2):
        for d in range(nz):
            arrived(orx.at[hb, d], osem.at[hb, d])

        @pl.when(h == 0)
        def _():
            arrived(pq.at[hb], bsem.at[hb])

        @pl.loop(0, nz)
        def _(back):
            zz = nz - 1 - back
            edges = zero8
            for k in reversed(range(nk)):
                kk = zz * nk + k
                mix = jnp.broadcast_to(mrx[zz, k:k + 1, :], (24, 128))
                nwt = -jnp.broadcast_to(mrx[zz, 8 + k:9 + k, :], (24, 128))
                keep = 1.0 - mix
                nxt = [ast[kk + 2, c, hb] for c in range(4)]
                a = [ast[kk + 1, c, hb] for c in range(4)]
                nw = orx[hb, zz, k, 3]
                r = [nw * (m - orx[hb, zz, k, c]) for c, m in enumerate(shear_of(nxt))]
                tilt = -0.5 * r[2]
                f = [
                    pq[hb, 0] - 0.5 * (r[0] + r[1]),
                    pq[hb, 1] + tilt,
                    pq[hb, 2] + tilt,
                    pq[hb, 3] - 0.5 * (r[0] - r[1]),
                ]
                d1, d2, off = mst[kk, 0, hb], mst[kk, 1, hb], mst[kk, 2, hb]
                pq[hb, 0] = d1 * f[0] + off * f[2] + pq[hb, 4]
                pq[hb, 1] = d1 * f[1] + off * f[3] + pq[hb, 5]
                pq[hb, 2] = off * f[0] + d2 * f[2] + pq[hb, 6]
                pq[hb, 3] = off * f[1] + d2 * f[3] + pq[hb, 7]
                for c in range(4):
                    pq[hb, 4 + c] = keep * f[c]
                c0 = unpack4(nwt * (f[0] * a[0] + f[1] * a[1]), sub)
                c1 = unpack4(nwt * (f[2] * a[2] + f[3] * a[3]), sub)
                c2 = unpack4(nwt * (f[0] * a[2] + f[1] * a[3] + f[2] * a[0] + f[3] * a[1]), sub)
                c0 = [jnp.where(inner, rows_of(t, -1), 0.0) for t in c0]
                c1 = [jnp.where(inner, rows_of(t, -1), 0.0) for t in c1]
                c2 = [jnp.where(inner, rows_of(t, -1), 0.0) for t in c2]
                l1, r1 = neighbours(c1, zero8, zero8, lane)
                l2, r2 = neighbours(c2, zero8, zero8, lane)
                for i in range(4):
                    q = 0.25 * (r2[i] - l2[i])
                    gsend[hb, zz, (i // 2) * tiles_of + 2 * k + i % 2] = (
                        rows_of(c0[i], 1) - 2.0 * c0[i] + rows_of(c0[i], -1)
                        + (r1[i] - 2.0 * c1[i] + l1[i])
                        + (rows_of(q, 1) - rows_of(q, -1))
                    )
                vl = c1[0] + 0.25 * (rows_of(c2[0], 1) - rows_of(c2[0], -1))
                vr = c1[3] - 0.25 * (rows_of(c2[3], 1) - rows_of(c2[3], -1))
                edges = jnp.where(lane == k, jnp.broadcast_to(vl[:, 0:1], (8, 128)), edges)
                edges = jnp.where(lane == 8 + k, jnp.broadcast_to(vr[:, 127:128], (8, 128)), edges)
            gsend[hb, zz, 2 * tiles_of] = edges
            send(*g_args(hb, zz))

        @pl.when(h == 1)
        def _():
            back_copy(hb).start()

    @pl.when(h == 1)
    def _():
        each(nz, send, stp_args)

        @pl.loop(0, nz)
        def _(away):
            send(*sta_args(near_first(away)))

    @pl.when((h == 0) & (z != 2))
    def _():
        send(*sta_args((z + 2) % nz))

    for hb in range(2):

        @pl.loop(0, nz)
        def _(away):
            c = near_first(away)
            arrived(gmid.at[hb, c], gsem.at[hb, c])
            for j in range(2):
                send(*f_args(hb, c, j))
                send(*fe_args(hb, c, j))

    each(ns, sent, pix_args)
    each(ns, sent, row_args)

    @pl.when(on_edge)
    def _():
        each(ns, sent, edge_args)

    each(nz, sent, meta_args)
    for hb in range(2):
        each(nz, sent, obs_args(hb))

    arrived(prow, rsem.at[1])
    arrived(stp, rsem.at[7])
    nchunk = 2 * nz

    @pl.loop(0, nchunk)
    def _(i):
        c = near_first(i // 2)
        hb = i % 2
        m = 2 * c + hb

        @pl.when(hb == 0)
        def _():
            arrived(sta.at[c], stsem.at[c])

        cp = ((m + nchunk - 1) % nchunk) // 2
        cn = ((m + 1) % nchunk) // 2
        tp = (4 * hb + 7) % 8
        tn = (4 * hb + 4) % 8
        y = []
        for b in range(2):
            t = [stp[c, b, 4 * hb + i] for i in range(4)]
            lf, rt = neighbours(
                t, cols_of(stp[cp, b, tp], -1), cols_of(stp[cn, b, tn], 1), lane
            )
            y.append([slopes(t[i], lf[i], rt[i]) for i in range(4)])
        ybefore, ynow = y
        before = [sta[c, 0, e, hb] for e in range(4)]
        now = [sta[c, 1, e, hb] for e in range(4)]
        for k in range(nk):
            mix3 = jnp.broadcast_to(msend[k:k + 1, :], (24, 128))
            wgt3 = jnp.broadcast_to(msend[8 + k:9 + k, :], (24, 128))
            mix, wgt = mix3[0:8], wgt3[0:8]
            keep3 = 1.0 - mix3
            keep = 1.0 - mix
            t = [
                prow[2 * m + i // 2, k, :, pl.ds(128 * (i % 2), 128)] for i in range(4)
            ]
            left = cols_of(prow[(2 * m + ns - 1) % ns, k, :, pl.ds(128, 128)], -1)
            right = cols_of(prow[(2 * m + 2) % ns, k, :, pl.ds(0, 128)], 1)
            lf, rt = neighbours(t, left, right, lane)
            b = [bends(t[i], lf[i], rt[i]) for i in range(4)]
            d1 = mix3 - wgt3 * pack4([x[0] for x in b], sub)
            d2 = mix3 - wgt3 * pack4([x[1] for x in b], sub)
            off = -wgt3 * pack4([x[2] for x in b], sub)
            new = step_forward(now, before, d1, d2, off, keep3)
            before, now = now, new
            for e, x in enumerate(shear_of(new)):
                for i, part in enumerate(unpack4(x, sub)):
                    col = pl.ds(pl.multiple_of(m * 512 + i * 128, 128), 128)
                    sv[k, e, :, col] = part[0:6]
            ynew = []
            for i in range(4):
                sl = slopes(t[i], lf[i], rt[i])
                both = []
                for e in range(2):
                    v = mix * ynow[i][e] + keep * ybefore[i][e] - wgt * sl[e]
                    both.append(v)
                    col = pl.ds(pl.multiple_of(m * 512 + i * 128, 128), 128)
                    dv[k, :, e, col] = v[0:6]
                ynew.append(both)
            ybefore, ynow = ynow, ynew

    arrived(grx, rsem.at[9])
    arrived(gerx, rsem.at[10])

    @pl.loop(0, nz)
    def _(zz):
        @pl.when((h == 1) | (zz > 0))
        def _():
            sent(*sta_args(zz))
            sent(*stp_args(zz))

        for hb in range(2):
            sent(*g_args(hb, zz))
            for j in range(2):
                sent(*f_args(hb, zz, j))
                sent(*fe_args(hb, zz, j))

    @pl.when(h == 0)
    def _():
        chain_copy(ast, 0, rsem.at[4]).wait_send()
        chain_copy(phi, 1, rsem.at[5]).wait_send()

    @pl.when(h == 1)
    def _():
        back_copy(0).wait_send()
        back_copy(1).wait_send()


def finish(nz, ns, nk, dv, sv, grx, gerx, defl, shear, grad, gv, sem):
    sub, lane = iotas()
    odd = lax.axis_index("slab") % 2
    out_s = pltpu.make_async_copy(sv, shear, sem.at[0])
    out_d = pltpu.make_async_copy(dv, defl, sem.at[1])
    out_g = pltpu.make_async_copy(gv, grad, sem.at[2])
    out_s.start()
    out_d.start()

    spot = lane == jnp.where(odd == 1, 127, 0)
    for k in range(nk):
        for t in range(2):
            part = []
            for d in range(ns):
                edge = jnp.broadcast_to(
                    jnp.where(odd == 1, gerx[d][:, k:k + 1], gerx[d][:, 8 + k:9 + k]), (8, 128)
                )
                part.append(grx[d, 2 * k + t] + jnp.where(spot & (odd == t), edge, 0.0))
            for d in range(ns):
                g = part[d]
                g = g + jnp.where(sub == 1, rows_of(part[(d + ns - 1) % ns], 6), 0.0)
                g = g + jnp.where(sub == 6, rows_of(part[(d + 1) % ns], -6), 0.0)
                gv[k, 6 * d:6 * d + 6, pl.ds(128 * t, 128)] = rows_of(g, 1)[0:6]
    out_g.start()
    out_s.wait()
    out_d.wait()
    out_g.wait()


def on_device(nz, ns, potential, mixing, lens_weight, observed, noise_weight):
    nk, total, width = potential.shape
    rows = total // ns
    wide = ns * width
    per = ns // nz
    last = nz * nk
    anyspec = pl.BlockSpec(memory_space=pl.ANY)
    hbm = pl.BlockSpec(memory_space=pltpu.HBM)
    vmem = pl.BlockSpec(memory_space=pltpu.VMEM)
    smem = pl.BlockSpec(memory_space=pltpu.SMEM)
    v = lambda *shape: pltpu.VMEM(shape, F32)
    dma = lambda *shape: pltpu.SemaphoreType.DMA(shape)
    received = [
        (nk, rows, 2, wide), (nk, 3, rows, wide), (ns, 2 * nk, 8, 128), (ns, 8, 128),
    ]
    stay = lambda x: pltpu.with_memory_space_constraint(x, pltpu.HBM)
    shaped = lambda shape: jax.ShapeDtypeStruct(shape, F32)
    mids = pl.pallas_call(
        functools.partial(exchange, nz, ns, nk),
        out_shape=tuple(shaped(x) for x in received),
        in_specs=[hbm] * 5,
        out_specs=(vmem,) * 4,
        scratch_shapes=[
            pltpu.SMEM((nk,), F32), pltpu.SMEM((nk,), F32),
            v(nk, total, width), v(nk, 3, rows, wide), v(nk, rows, wide),
            v(ns, nk, 8, width), v(ns, 8, 128), v(2, nz, nk, 4, 24, 128),
            v(ns, nk, 8, width), v(nz, 2, 4, 2, 24, 128), v(nz, 2, 8, 8, 128), v(16, 128),
            v(nz, per, nk, 8, width), v(nz, 2, 8, 128), v(nz, 16, 128), v(2, nz, nk, 4, 24, 128),
            v(last + 2, 4, 2, 24, 128), v(last, 3, 2, 24, 128), v(last + 2, 8, 8, 128),
            v(2, 8, 24, 128),
            v(2, nz, 4 * nk + 1, 8, 128), v(2, nz, 4 * nk + 1, 8, 128),
            dma(6), dma(2, ns), dma(ns), dma(nz), dma(2, nz), dma(nz), dma(nz), dma(4),
            dma(2, nz), dma(2, nz, 2), dma(2, nz, 2), dma(11), dma(2, nz), dma(2, nz), dma(2), dma(nz),
            pltpu.SemaphoreType.REGULAR,
        ],
        name="exchange",
        compiler_params=pltpu.CompilerParams(
            collective_id=0, has_side_effects=True, vmem_limit_bytes=24 * 1024 * 1024
        ),
    )(stay(potential), stay(mixing), stay(lens_weight), stay(observed), stay(noise_weight))
    defl, shear, grad = pl.pallas_call(
        functools.partial(finish, nz, ns, nk),
        out_shape=(
            shaped((nk, rows, 2, wide)), shaped((nk, 3, rows, wide)), shaped((nk, total, width)),
        ),
        in_specs=[vmem] * 4,
        out_specs=(hbm,) * 3,
        scratch_shapes=[v(nk, total, width), dma(3)],
        name="finish",
        compiler_params=pltpu.CompilerParams(vmem_limit_bytes=24 * 1024 * 1024),
    )(*mids)
    return jnp.transpose(defl, (0, 2, 1, 3)), shear, grad


def solution(mesh):
    nz = mesh.shape["plane"] // NH
    ns = mesh.shape["slab"]
    placed = (
        P("plane", None, "slab"),
        P("plane"),
        P("plane"),
        P("plane", None, "slab", None),
        P("plane", "slab", None),
    )
    return jax.shard_map(
        functools.partial(on_device, nz, ns),
        mesh=mesh,
        in_specs=placed,
        out_specs=(
            P("plane", None, "slab", None),
            P("plane", None, "slab", None),
            P("plane", None, "slab"),
        ),
        check_vma=False,
    )
```
